512 devices in a mesh: slab: 32 (over x, y, core), pencil: 16 (over z).
Axes of the slice: x: 4, y: 4, z: 16, core: 2. Of those that a mesh axis runs over, the one named last changes fastest.
Arguments:
- orbitals: float32 [4, 192, 192, 192], P(None, 'slab', 'pencil'), may hold values from -6 to 6
- potential: float32 [192, 192, 192], P('slab', 'pencil'), may hold values from 0.5 to 2.5
- unlocked: int32 [4], replicated, may hold values 0 or 1
Outputs:
- orthonormal: float32 [4, 192, 192, 192], P(None, 'slab', 'pencil')
The draws below stay inside these ranges and needn't reach their ends.
Inputs may be any that keep to these rules, and one draw needn't show every extreme that they name: `unlocked`: 1 marks a band that is filtered, 0 a locked band kept as it is.
All inputs are finite; a program needn't handle non-finite values.
Results may differ from the reference program's by a relative error of at most 0.00005.
Values sent between devices are 32-bit elements; how exact they have to be, the bound alone decides.
No kernel may reach another device: no remote copies, remote signals or barrier semaphores. Data moves between devices by JAX's collectives and lax.ppermute only.
A program may use at most 64 MiB of HBM per device.

```python
import jax
import jax.numpy as jnp
from jax import lax

NG = 192
NB = 4


def draw_orbitals(key, part):
    weight_key = jax.random.fold_in(key, 11)
    common_key = jax.random.fold_in(key, 12)
    private_key = jax.random.fold_in(key, 13)
    weights = jax.random.uniform(weight_key, (NB,), jnp.float32, 0.5, 0.9)
    common = jax.random.normal(common_key, (NG, NG, NG), jnp.float32)
    private = jax.random.normal(private_key, (NB, NG, NG, NG), jnp.float32)
    values = weights[:, None, None, None] * common[None] + private
    return jnp.clip(values, -6.0, 6.0).astype(jnp.float32)


def plant(drawn, rng, smallest, largest):
    shape = drawn.shape
    place = [jax.random.randint(jax.random.fold_in(rng, axis), (), 0, shape[axis]) for axis in range(len(shape))]
    drawn = drawn.at[tuple(place)].set(smallest)
    longest = shape.index(max(shape))
    place[longest] = (place[longest] + 1) % shape[longest]
    return drawn.at[tuple(place)].set(largest)


def level_of(key, extent, shards, least, top_value):
    level = 1.0
    for dim, blocks in shards:
        heights = jax.random.uniform(jax.random.fold_in(jax.random.fold_in(key, 6), dim), (blocks,), jnp.float32, least / len(shards), top_value / len(shards))
        level = level * jnp.repeat(jnp.exp(heights), extent[dim] // blocks).reshape((-1,) + (1,) * (len(extent) - 1 - dim))
    return level


def setup_inputs(seed: int = 0) -> dict:
    keys = jax.random.split(jax.random.key(seed), 4)
    return {
        "orbitals": draw_orbitals(jax.random.fold_in(keys[3], 71), 0),
        "potential": jnp.clip(0.5 + 2.0 * jax.random.uniform(keys[1], (NG, NG, NG), jnp.float32) ** level_of(keys[1], (NG, NG, NG), ((0, 32), (1, 16)), -0.2, 0.2), 0.5, 2.5),
        "unlocked": plant((jax.random.randint(keys[2], (NB,), 0, 4) < 3).astype(jnp.int32), jax.random.fold_in(keys[2], 1), 0, 1),
    }


kinetic_scale = 4.0
filter_center = 1.0
filter_half = 1.5

def kinetic_table():
    index = jnp.arange(NG)
    modes = jnp.where(index < NG // 2, index, index - NG).astype(jnp.float32)
    squared = modes[:, None, None] ** 2 + modes[None, :, None] ** 2 + modes[None, None, :] ** 2
    radius = float((NG // 4) ** 2)
    return jnp.where(squared < radius, kinetic_scale * squared / radius, 0.0)

def reference(orbitals, potential, unlocked):
    kinetic = kinetic_table().astype(orbitals.dtype)

    def apply_one(orbital):
        spectrum = jnp.fft.fftn(orbital)
        kinetic_part = jnp.real(jnp.fft.ifftn(spectrum * kinetic)).astype(orbital.dtype)
        return kinetic_part + potential * orbital
    applied = lax.map(apply_one, orbitals)
    filtered = jnp.where(unlocked[:, None, None, None] == 1, (applied - filter_center * orbitals) / filter_half, orbitals)
    flattened = filtered.reshape(NB, -1)
    intersection = jnp.dot(flattened, flattened.T, precision=lax.Precision.HIGHEST) / float(NG ** 3)
    factor = jnp.linalg.cholesky(intersection)
    result = jax.scipy.linalg.solve_triangular(factor, flattened, lower=True)
    return result.reshape(orbitals.shape)
```

```python
import functools

import jax
import jax.numpy as jnp
import numpy as np
from jax import lax
from jax.experimental import pallas as pl
from jax.experimental.pallas import tpu as pltpu
from jax.sharding import PartitionSpec as P

NG = 192
NB = 4
CUT = NG // 4
MODES = 2 * CUT
SLAB = 32
PENCIL = 16
ROWS = NG // SLAB
COLS = NG // PENCIL
CELLS = float(NG**3)
THIRDS = MODES // SLAB
FIRSTS = MODES // PENCIL
PAIRS = [(a, b) for a in range(NB) for b in range(a + 1)]
highest = lax.Precision.HIGHEST


def basis():
    place = np.arange(NG)
    mode = np.arange(MODES)
    angle = 2.0 * np.pi / NG * ((mode[:, None] % CUT) * place[None, :] % NG)
    return np.where(mode[:, None] < CUT, np.cos(angle), np.sin(angle))


def tables():
    real = basis()
    third = real
    first = np.zeros((PENCIL, 8, SLAB, 8))
    first[:, :FIRSTS, :, :ROWS] = real.reshape(PENCIL, FIRSTS, SLAB, ROWS)
    first = first.reshape(PENCIL * 8, SLAB * 8)
    second = np.zeros((128, PENCIL, 16))
    second[:MODES, :, :COLS] = real.reshape(MODES, PENCIL, COLS)
    second = second.reshape(128, PENCIL * 16)
    third_back = real.reshape(SLAB, THIRDS, NG).transpose(1, 0, 2).reshape(MODES, NG)
    made = (third, first, first.T, second.T, second, third_back)
    return [np.ascontiguousarray(t, dtype=np.float32) for t in made]


def dot(a, b, dims=((1,), (0,))):
    return lax.dot_general(a, b, (dims, ((), ())), precision=highest, preferred_element_type=jnp.float32)


def local_part(flag, orbital, shifted):
    return jnp.where(flag == 1, orbital * shifted * (1.0 / 1.5), orbital)


def forward_third(flags, orbitals, potential, table, out, sums, lines):
    empty = jnp.zeros((16 - COLS, NG), jnp.float32)
    totals = [None] * len(PAIRS)
    for i in range(ROWS):
        shifted = potential[i] - 1.0
        for b in range(NB):
            base = i * 128 + b * 16
            value = orbitals[b, i]
            lines[base : base + COLS, :] = value
            lines[base + COLS : base + 16, :] = empty
            lines[base + 64 : base + 64 + COLS, :] = local_part(flags[b], value, shifted)
            lines[base + 64 + COLS : base + 80, :] = empty
        own = [lines[i * 128 + 64 + b * 16 : i * 128 + 80 + b * 16, :] for b in range(NB)]
        for q, (a, b) in enumerate(PAIRS):
            term = own[a] * own[b]
            totals[q] = term if totals[q] is None else totals[q] + term
    for q in range(len(PAIRS)):
        sums[q * 8 : q * 8 + 8, :] = totals[q][:8] + totals[q][8:]
    spectrum = dot(table[...], lines[...], ((1,), (1,)))
    for i in range(ROWS):
        out[pl.ds(i, MODES, stride=8), :] = spectrum[:, i * 128 : i * 128 + 128]
    for i in range(ROWS, 8):
        out[pl.ds(i, MODES, stride=8), :] = jnp.zeros((MODES, 128), jnp.float32)


def forward_first(given, table, out):
    for t in range(THIRDS):
        block = given[:, t * 8 : t * 8 + 8, :].reshape(SLAB * 8, 128)
        out[:, t * 8 : t * 8 + 8, :] = dot(table[...], block).reshape(PENCIL, 8, 128)


def middle(flags, places, given, sums, forward, back, out, lines):
    for p in range(PENCIL):
        for u in range(2 * NB):
            lines[u * 24 : u * 24 + 24, p * 16 : p * 16 + 16] = given[p, :, u * 16 : u * 16 + 16]
    spectrum = dot(lines[...], forward[...])
    row = lax.broadcasted_iota(jnp.int32, (24, 128), 0)
    lane = lax.broadcasted_iota(jnp.int32, (24, 128), 1)
    third = THIRDS * places[0] + row // 8
    first = FIRSTS * places[1] + row % 8
    known = (row % 8 < FIRSTS) & (lane < MODES)
    squared = jnp.zeros((24, 128), jnp.int32)
    weight = jnp.full((24, 128), 1.0 / CELLS, jnp.float32)
    for mode in (third, first, lane):
        size = jnp.where(mode < CUT, mode, mode - CUT)
        squared = squared + size * size
        weight = weight * jnp.where(mode == 0, 1.0, jnp.where(mode == CUT, 0.0, 2.0))
    kinetic = squared.astype(jnp.float32) * (4.0 / CUT**2)
    kinetic = jnp.where(known & (squared < CUT * CUT), kinetic, 0.0)
    weight = weight * kinetic
    scaled, other = [], []
    for b in range(NB):
        alpha = jnp.where(flags[b] == 1, 1.0 / 1.5, 0.0)
        value = spectrum[b * 24 : b * 24 + 24] * alpha
        scaled.append(value * weight)
        other.append(0.5 * kinetic * value + spectrum[(NB + b) * 24 : (NB + b) * 24 + 24])
    returned = dot(jnp.concatenate(scaled, axis=0), back[...])
    for p in range(PENCIL):
        for b in range(NB):
            for t in range(THIRDS):
                at = (t % 2) * 64 + b * 16
                out[p, (t // 2) * 8 : (t // 2) * 8 + 8, at : at + 16] = returned[
                    b * 24 + t * 8 : b * 24 + t * 8 + 8, p * 16 : p * 16 + 16
                ]
    values = []
    for q, (a, b) in enumerate(PAIRS):
        term = scaled[a] * other[b] + scaled[b] * other[a]
        term = term[:8] + term[8:16] + term[16:]
        mine = sums[q * 8 : q * 8 + 8, :]
        total = jnp.sum(term, axis=1, keepdims=True) + jnp.sum(mine, axis=1, keepdims=True)
        values.append(jnp.sum(total, axis=0, keepdims=True))
    row = lax.broadcasted_iota(jnp.int32, (8, 64), 0)
    lane = lax.broadcasted_iota(jnp.int32, (8, 64), 1)
    note = jnp.zeros((8, 64), jnp.float32)
    for q, value in enumerate(values):
        note = jnp.where((row == q % 8) & (lane == q // 8), value, note)
    for p in range(PENCIL):
        out[p, 8:16, 64:128] = note


def back_first(given, table, out):
    low = given[:, 0:8, :].reshape(PENCIL * 8, 128)
    high = given[:, 8:16, :].reshape(PENCIL * 8, 128)
    note = given[0, 8:16, :]
    for p in range(1, PENCIL):
        note = note + given[p, 8:16, :]
    out[:, 0:8, :] = dot(table[...], low).reshape(SLAB, 8, 128)
    lane = lax.broadcasted_iota(jnp.int32, (SLAB, 8, 128), 2)
    out[:, 8:16, :] = jnp.where(lane >= 64, note[None], dot(table[...], high).reshape(SLAB, 8, 128))


def back_third(flags, orbitals, potential, given, table, out, lines):
    for i in range(ROWS):
        low = given[pl.ds(i, SLAB, stride=16), :]
        high = given[pl.ds(8 + i, SLAB, stride=16), :]
        lines[0:32, i * 64 : i * 64 + 64] = low[:, :64]
        lines[32:64, i * 64 : i * 64 + 64] = low[:, 64:]
        lines[64:96, i * 64 : i * 64 + 64] = high[:, :64]
    kinetic_part = dot(lines[...], table[...], ((0,), (0,)))
    note = given[8:16, :]
    for s in range(1, SLAB):
        note = note + given[s * 16 + 8 : s * 16 + 16, :]
    note = note * (1.0 / CELLS)
    entry = {}
    for q, pair in enumerate(PAIRS):
        at = 64 + q // 8
        entry[pair] = note[q % 8 : q % 8 + 1, at : at + 1]
    factor, inverse = {}, {}
    for a in range(NB):
        for b in range(a + 1):
            value = entry[a, b]
            for c in range(b):
                value = value - factor[a, c] * factor[b, c]
            if a == b:
                factor[a, a] = jnp.sqrt(value)
                inverse[a] = 1.0 / factor[a, a]
            else:
                factor[a, b] = value * inverse[b]
    for i in range(ROWS):
        shifted = potential[i] - 1.0
        done = []
        for a in range(NB):
            value = local_part(flags[a], orbitals[a, i], shifted)
            value = value + kinetic_part[i * 64 + a * 16 : i * 64 + a * 16 + COLS]
            for b in range(a):
                value = value - factor[a, b] * done[b]
            value = value * inverse[a]
            done.append(value)
            out[a, i] = value


def smem():
    return pl.BlockSpec(memory_space=pltpu.SMEM)


def vmem():
    return pl.BlockSpec(memory_space=pltpu.VMEM)


def f32(*shape):
    return jax.ShapeDtypeStruct(shape, jnp.float32)


def call(body, kinds, outs, scratch=()):
    return pl.pallas_call(
        body,
        out_shape=outs,
        in_specs=[smem() if kind == "s" else vmem() for kind in kinds],
        out_specs=jax.tree.map(lambda _: vmem(), outs),
        scratch_shapes=[pltpu.VMEM(shape, jnp.float32) for shape in scratch],
        name=body.__name__,
    )


def steps():
    third, first, first_back, second, second_back, third_back = tables()

    def one(flags, orbitals, potential):
        made = call(forward_third, "svvv", (f32(MODES * 8, 128), f32(8 * len(PAIRS), NG)), [(ROWS * 128, NG)])
        spectrum, sums = made(flags, orbitals, potential, third)
        return spectrum.reshape(SLAB, 24, 128), sums

    def two(given):
        return call(forward_first, "vv", f32(PENCIL, 24, 128))(given, first)

    def three(flags, places, given, sums):
        made = call(middle, "ssvvvv", f32(PENCIL, 16, 128), [(8 * 24, PENCIL * 16)])
        return made(flags, places, given, sums, second, second_back)

    def four(given):
        return call(back_first, "vv", f32(SLAB, 16, 128))(given, first_back)

    def five(flags, orbitals, potential, given):
        made = call(back_third, "svvvv", f32(NB, ROWS, COLS, NG), [(MODES, ROWS * 64)])
        return made(flags, orbitals, potential, given.reshape(SLAB * 16, 128), third_back)

    return one, two, three, four, five


def local(orbitals, potential, unlocked):
    one, two, three, four, five = steps()
    trade = functools.partial(lax.all_to_all, split_axis=0, concat_axis=0, tiled=True)
    places = jnp.stack([lax.axis_index("slab"), lax.axis_index("pencil")]).astype(jnp.int32)
    spectrum, sums = one(unlocked, orbitals, potential)
    spectrum = two(trade(spectrum, "slab"))
    spectrum = three(unlocked, places, trade(spectrum, "pencil"), sums)
    spectrum = four(trade(spectrum, "pencil"))
    return five(unlocked, orbitals, potential, trade(spectrum, "slab"))


def solution(mesh):
    in_specs = (P(None, "slab", "pencil", None), P("slab", "pencil", None), P())
    out_specs = P(None, "slab", "pencil", None)
    return jax.shard_map(local, mesh=mesh, in_specs=in_specs, out_specs=out_specs, check_vma=False)
```

```python
import functools

import jax
import jax.numpy as jnp
import numpy as np
from jax import lax
from jax.experimental import pallas as pl
from jax.experimental.pallas import tpu as pltpu
from jax.sharding import PartitionSpec as P

NG = 192
NB = 4
CUT = NG // 4
MODES = 2 * CUT
SLAB = 32
PENCIL = 16
ROWS = NG // SLAB
COLS = NG // PENCIL
CELLS = float(NG**3)
THIRDS = MODES // SLAB
FIRSTS = MODES // PENCIL
WIDE = 2 * NB * COLS
HALF = NB * COLS
PAIRS = [(a, b) for a in range(NB) for b in range(a + 1)]
highest = lax.Precision.HIGHEST


def basis():
    place = np.arange(NG)
    mode = np.arange(MODES)
    angle = 2.0 * np.pi / NG * ((mode[:, None] % CUT) * place[None, :] % NG)
    return np.where(mode[:, None] < CUT, np.cos(angle), np.sin(angle))


def tables():
    real = basis()
    third = real.reshape(SLAB, THIRDS, NG).transpose(1, 0, 2).reshape(MODES, NG)
    first = np.zeros((PENCIL, 8, SLAB, 8))
    first[:, :FIRSTS, :, :ROWS] = real.reshape(PENCIL, FIRSTS, SLAB, ROWS)
    first = first.reshape(PENCIL * 8, SLAB * 8)
    second = np.zeros((128, NG))
    second[:MODES] = real
    made = (third, first, first.T, second.T, second)
    return [np.ascontiguousarray(t, dtype=np.float32) for t in made]


def dot(a, b, dims=((1,), (0,))):
    return lax.dot_general(a, b, (dims, ((), ())), precision=highest, preferred_element_type=jnp.float32)


def lanes(*shape):
    return lax.broadcasted_iota(jnp.int32, shape, len(shape) - 1)


def turn(value, by):
    by = by % 128
    return pltpu.roll(value, by, 1) if by else value


def gathered(pieces, width, start):
    lane = lanes(*pieces[0].shape)
    result = jnp.zeros(pieces[0].shape, jnp.float32)
    for k, piece in enumerate(pieces):
        here = (lane >= k * width) & (lane < k * width + width)
        result = jnp.where(here, turn(piece, k * width - start), result)
    return result


def forward_third(flags, orbitals, potential, table, out, local, sums, lines):
    totals = [None] * len(PAIRS)
    for i in range(ROWS):
        shifted = (potential[i] - 1.0) * (1.0 / 1.5)
        own = []
        for b in range(NB):
            base = i * 128 + b * COLS
            value = orbitals[i, :, b, :]
            kept = jnp.where(flags[b] == 1, value * shifted, value)
            lines[base : base + COLS, :] = value
            lines[base + HALF : base + HALF + COLS, :] = kept
            local[b, i] = kept
            own.append(kept)
        for q, (a, b) in enumerate(PAIRS):
            term = own[a] * own[b]
            totals[q] = term if totals[q] is None else totals[q] + term
    sums[...] = jnp.zeros_like(sums)
    for q in range(len(PAIRS)):
        sums[q : q + 1, :] = jnp.sum(totals[q], axis=0, keepdims=True)
    spectrum = dot(table[...], lines[...], ((1,), (1,)))
    whole = lanes(SLAB, 128)
    last = []
    for i in range(ROWS):
        parts = [spectrum[t * 32 : t * 32 + 32, i * 128 : i * 128 + 128] for t in range(THIRDS)]
        for t in range(2):
            extra = turn(parts[2], WIDE - 32 * t)
            out[pl.ds(t * 8 + i, SLAB, stride=16), :] = jnp.where(whole < WIDE, parts[t], extra)
        last.append(parts[2])
    for t in range(2):
        out[pl.ds(t * 8 + 6, SLAB, stride=16), :] = gathered(last[t * 4 : t * 4 + 4], 32, 64)
        out[pl.ds(t * 8 + 7, SLAB, stride=16), :] = jnp.zeros((SLAB, 128), jnp.float32)


def forward_first(given, table, out, taken, made):
    rest = [given[pl.ds(t * 8 + 6, SLAB, stride=16), :] for t in range(2)]
    for i in range(8):
        value = turn(rest[i // 4], -32 * (i % 4)) if i < ROWS else jnp.zeros((SLAB, 128), jnp.float32)
        taken[pl.ds(i, SLAB, stride=8), :] = value
    tiles = given[...].reshape(SLAB, 16, 128)
    for t in range(2):
        block = tiles[:, t * 8 : t * 8 + 8].reshape(SLAB * 8, 128)
        result = dot(table[...], block)
        for p in range(PENCIL):
            out[p * 16 + t * 8 : p * 16 + t * 8 + 8, :] = result[p * 8 : p * 8 + 8]
    made[...] = dot(table[...], taken[...])
    pieces = [made[pl.ds(i, PENCIL, stride=8), :] for i in range(FIRSTS)]
    for t in range(2):
        out[pl.ds(t * 8 + 6, PENCIL, stride=16), :] = gathered(pieces[t * 4 : t * 4 + 4], 32, 0)


def middle(flags, given, sums, forward, back, out, third, lines, wide, more, rows):
    rest = [given[pl.ds(t * 8 + 6, PENCIL, stride=16), :] for t in range(2)]
    for i in range(8):
        value = turn(rest[i // 4], 64 - 32 * (i % 4)) if i < FIRSTS else jnp.zeros((PENCIL, 128), jnp.float32)
        third[pl.ds(i, PENCIL, stride=8), :] = value
    lane = lanes(8, 128)
    for p in range(PENCIL):
        parts = [given[p * 16 : p * 16 + 8, :], given[p * 16 + 8 : p * 16 + 16, :]]
        last = jnp.where(lane < 64, turn(parts[1], 64), third[p * 8 : p * 8 + 8, :])
        parts.append(jnp.where(lane < 32, turn(parts[0], 32), last))
        for u in range(2 * NB):
            for t in range(THIRDS):
                at = u * 24 + t * 8
                lines[at : at + 8, p * COLS : p * COLS + COLS] = parts[t][:, u * COLS : u * COLS + COLS]
    spectrum = dot(lines[...], forward[...])
    row = lax.broadcasted_iota(jnp.int32, (24, 128), 0)
    lane = lanes(24, 128)
    third_mode = THIRDS * lax.axis_index("slab") + row // 8
    first_mode = FIRSTS * lax.axis_index("pencil") + row % 8
    known = (row % 8 < FIRSTS) & (lane < MODES)
    squared = jnp.zeros((24, 128), jnp.int32)
    weight = jnp.full((24, 128), 1.0 / CELLS, jnp.float32)
    for mode in (third_mode, first_mode, lane):
        size = jnp.where(mode < CUT, mode, mode - CUT)
        squared = squared + size * size
        weight = weight * jnp.where(mode == 0, 1.0, jnp.where(mode == CUT, 0.0, 2.0))
    kinetic = squared.astype(jnp.float32) * (4.0 / CUT**2)
    kinetic = jnp.where(known & (squared < CUT * CUT), kinetic, 0.0)
    weight = weight * kinetic
    scaled, other = [], []
    for b in range(NB):
        alpha = jnp.where(flags[b] == 1, 1.0 / 1.5, 0.0)
        value = spectrum[b * 24 : b * 24 + 24] * alpha
        scaled.append(value * weight)
        other.append(0.5 * kinetic * value + spectrum[(NB + b) * 24 : (NB + b) * 24 + 24])
    returned = dot(jnp.concatenate(scaled, axis=0), back[...])
    rows[...] = jnp.zeros_like(rows)
    for q, (a, b) in enumerate(PAIRS):
        term = scaled[a] * other[b] + scaled[b] * other[a]
        rows[q : q + 1, :] = jnp.sum(term[:8] + term[8:16] + term[16:], axis=0, keepdims=True)
    total = jnp.sum(rows[...], axis=1, keepdims=True) + jnp.sum(sums[...], axis=1, keepdims=True)
    picked = lax.broadcasted_iota(jnp.int32, (16, 128), 0) == lanes(16, 128)
    note = jnp.sum(jnp.where(picked, total, 0.0), axis=0, keepdims=True)
    for p in range(PENCIL):
        for b in range(NB):
            for t in range(THIRDS):
                at = t * HALF + b * COLS
                wide[p * 8 : p * 8 + 8, at : at + COLS] = returned[b * 24 + t * 8 : b * 24 + t * 8 + 8, p * COLS : p * COLS + COLS]
    more[...] = wide[:, 128:256]
    out[...] = wide[:, 0:128]
    pieces = [more[pl.ds(i, PENCIL, stride=8), :] for i in range(FIRSTS)]
    out[pl.ds(6, PENCIL, stride=8), :] = gathered(pieces, 16, 0)
    out[pl.ds(7, PENCIL, stride=8), :] = jnp.broadcast_to(note, (PENCIL, 128))


def back_first(given, table, out, taken, made):
    rest = given[pl.ds(6, PENCIL, stride=8), :]
    for i in range(8):
        value = turn(rest, -16 * i) if i < FIRSTS else jnp.zeros((PENCIL, 128), jnp.float32)
        taken[pl.ds(i, PENCIL, stride=8), :] = value
    out[...] = dot(table[...], given[...])
    made[...] = dot(table[...], taken[...])
    pieces = [made[pl.ds(i, SLAB, stride=8), :] for i in range(ROWS)]
    out[pl.ds(6, SLAB, stride=8), :] = gathered(pieces, 16, 0)
    note = jnp.sum(given[pl.ds(7, PENCIL, stride=8), :], axis=0, keepdims=True)
    out[pl.ds(7, SLAB, stride=8), :] = jnp.broadcast_to(note, (SLAB, 128))


def back_third(given, local, table, out, lines):
    rest = given[pl.ds(6, SLAB, stride=8), :]
    for i in range(ROWS):
        value = given[pl.ds(i, SLAB, stride=8), :]
        at = i * HALF
        lines[0:32, at : at + HALF] = value[:, :HALF]
        lines[32:64, at : at + HALF] = value[:, HALF:WIDE]
        lines[64:96, at : at + 32] = value[:, WIDE:128]
        lines[64:96, at + 32 : at + HALF] = rest[:, 16 * i : 16 * i + 16]
    kinetic_part = dot(lines[...], table[...], ((0,), (0,)))
    note = jnp.sum(given[pl.ds(7, SLAB, stride=8), :], axis=0, keepdims=True) * (1.0 / CELLS)
    factor, inverse = {}, {}
    for q, (a, b) in enumerate(PAIRS):
        value = note[:, q : q + 1]
        for c in range(b):
            value = value - factor[a, c] * factor[b, c]
        if a == b:
            factor[a, a] = jnp.sqrt(value)
            inverse[a] = 1.0 / factor[a, a]
        else:
            factor[a, b] = value * inverse[b]
    for i in range(ROWS):
        done = []
        for a in range(NB):
            value = local[a, i] + kinetic_part[i * HALF + a * COLS : i * HALF + a * COLS + COLS]
            for b in range(a):
                value = value - factor[a, b] * done[b]
            value = value * inverse[a]
            done.append(value)
            out[i, :, a, :] = value


def smem():
    return pl.BlockSpec(memory_space=pltpu.SMEM)


def vmem():
    return pl.BlockSpec(memory_space=pltpu.VMEM)


def f32(*shape):
    return jax.ShapeDtypeStruct(shape, jnp.float32)


def call(body, kinds, outs, scratch=()):
    return pl.pallas_call(
        body,
        out_shape=outs,
        in_specs=[smem() if kind == "s" else vmem() for kind in kinds],
        out_specs=jax.tree.map(lambda _: vmem(), outs),
        scratch_shapes=[pltpu.VMEM(shape, jnp.float32) for shape in scratch],
        name=body.__name__,
    )


def trade(value, axis, number):
    blocks = value.reshape(number, -1, 128)
    return lax.all_to_all(blocks, axis, split_axis=0, concat_axis=0, tiled=True).reshape(value.shape)


def local_step(orbitals, potential, unlocked):
    third, first, first_back, second, second_back = tables()
    outs = (f32(SLAB * 16, 128), f32(NB, ROWS, COLS, NG), f32(16, NG))
    made = call(forward_third, "svvv", outs, [(ROWS * 128, NG)])
    spectrum, local, sums = made(unlocked, orbitals.transpose(1, 2, 0, 3), potential, third)
    spectrum = trade(spectrum, "slab", SLAB)
    made = call(forward_first, "vv", f32(PENCIL * 16, 128), [(SLAB * 8, 128), (PENCIL * 8, 128)])
    spectrum = trade(made(spectrum, first), "pencil", PENCIL)
    scratch = [(PENCIL * 8, 128), (8 * 24, NG), (PENCIL * 8, 256), (PENCIL * 8, 128), (16, 128)]
    made = call(middle, "svvvv", f32(PENCIL * 8, 128), scratch)
    spectrum = trade(made(unlocked, spectrum, sums, second, second_back), "pencil", PENCIL)
    made = call(back_first, "vv", f32(SLAB * 8, 128), [(PENCIL * 8, 128), (SLAB * 8, 128)])
    spectrum = trade(made(spectrum, first_back), "slab", SLAB)
    made = call(back_third, "vvv", f32(ROWS, COLS, NB, NG), [(MODES, ROWS * HALF)])
    return made(spectrum, local, third).transpose(2, 0, 1, 3)


def solution(mesh):
    in_specs = (P(None, "slab", "pencil", None), P("slab", "pencil", None), P())
    out_specs = P(None, "slab", "pencil", None)
    return jax.shard_map(local_step, mesh=mesh, in_specs=in_specs, out_specs=out_specs, check_vma=False)
```

```python
import functools

import jax
import jax.numpy as jnp
import numpy as np
from jax import lax
from jax.experimental import pallas as pl
from jax.experimental.pallas import tpu as pltpu
from jax.sharding import PartitionSpec as P

NG = 192
NB = 4
CUT = NG // 4
MODES = 2 * CUT
SLAB = 32
PENCIL = 16
ROWS = NG // SLAB
COLS = NG // PENCIL
CELLS = float(NG**3)
THIRDS = MODES // SLAB
FIRSTS = MODES // PENCIL
WIDE = 2 * NB * COLS
HALF = NB * COLS
PAIRS = [(a, b) for a in range(NB) for b in range(a + 1)]
highest = lax.Precision.HIGHEST


def basis():
    place = np.arange(NG)
    mode = np.arange(MODES)
    angle = 2.0 * np.pi / NG * ((mode[:, None] % CUT) * place[None, :] % NG)
    return np.where(mode[:, None] < CUT, np.cos(angle), np.sin(angle))


def tables():
    real = basis()
    third = real.reshape(SLAB, THIRDS, NG).transpose(1, 0, 2).reshape(MODES, NG)
    first = np.zeros((PENCIL, 8, SLAB, 8))
    first[:, :FIRSTS, :, :ROWS] = real.reshape(PENCIL, FIRSTS, SLAB, ROWS)
    first = first.reshape(PENCIL * 8, SLAB * 8)
    second = np.zeros((128, NG))
    second[:MODES] = real
    made = (third, first, first.T, second.T, second)
    return [np.ascontiguousarray(t, dtype=np.float32) for t in made]


def dot(a, b, dims=((1,), (0,))):
    return lax.dot_general(a, b, (dims, ((), ())), precision=highest, preferred_element_type=jnp.float32)


def lanes(*shape):
    return lax.broadcasted_iota(jnp.int32, shape, len(shape) - 1)


def turn(value, by):
    by = by % 128
    return pltpu.roll(value, by, 1) if by else value


def gathered(pieces, width, start):
    lane = lanes(*pieces[0].shape)
    result = jnp.zeros(pieces[0].shape, jnp.float32)
    for k, piece in enumerate(pieces):
        here = (lane >= k * width) & (lane < k * width + width)
        result = jnp.where(here, turn(piece, k * width - start), result)
    return result


def forward_third(flags, orbitals, potential, table, out, local, sums, lines):
    totals = [None] * len(PAIRS)
    for i in range(ROWS):
        shifted = (potential[i] - 1.0) * (1.0 / 1.5)
        own = []
        for b in range(NB):
            base = i * 128 + b * COLS
            value = orbitals[i, :, b, :]
            kept = jnp.where(flags[b] == 1, value * shifted, value)
            lines[base : base + COLS, :] = value
            lines[base + HALF : base + HALF + COLS, :] = kept
            local[b, i] = kept
            own.append(kept)
        for q, (a, b) in enumerate(PAIRS):
            term = own[a] * own[b]
            totals[q] = term if totals[q] is None else totals[q] + term
    sums[...] = jnp.zeros_like(sums)
    for q in range(len(PAIRS)):
        sums[q : q + 1, :] = jnp.sum(totals[q], axis=0, keepdims=True)
    spectrum = dot(table[...], lines[...], ((1,), (1,)))
    whole = lanes(SLAB, 128)
    last = []
    for i in range(ROWS):
        parts = [spectrum[t * 32 : t * 32 + 32, i * 128 : i * 128 + 128] for t in range(THIRDS)]
        for t in range(2):
            extra = turn(parts[2], WIDE - 32 * t)
            out[pl.ds(t * 8 + i, SLAB, stride=16), :] = jnp.where(whole < WIDE, parts[t], extra)
        last.append(parts[2])
    for t in range(2):
        out[pl.ds(t * 8 + 6, SLAB, stride=16), :] = gathered(last[t * 4 : t * 4 + 4], 32, 64)
        out[pl.ds(t * 8 + 7, SLAB, stride=16), :] = jnp.zeros((SLAB, 128), jnp.float32)


def forward_first(given, table, out, taken, made):
    rest = [given[pl.ds(t * 8 + 6, SLAB, stride=16), :] for t in range(2)]
    for i in range(8):
        value = turn(rest[i // 4], -32 * (i % 4)) if i < ROWS else jnp.zeros((SLAB, 128), jnp.float32)
        taken[pl.ds(i, SLAB, stride=8), :] = value
    tiles = given[...].reshape(SLAB, 16, 128)
    for t in range(2):
        block = tiles[:, t * 8 : t * 8 + 8].reshape(SLAB * 8, 128)
        result = dot(table[...], block)
        for p in range(PENCIL):
            out[p * 16 + t * 8 : p * 16 + t * 8 + 8, :] = result[p * 8 : p * 8 + 8]
    made[...] = dot(table[...], taken[...])
    pieces = [made[pl.ds(i, PENCIL, stride=8), :] for i in range(FIRSTS)]
    for t in range(2):
        out[pl.ds(t * 8 + 6, PENCIL, stride=16), :] = gathered(pieces[t * 4 : t * 4 + 4], 32, 0)


def middle(flags, given, sums, forward, back, out, third, lines, wide, more, rows):
    rest = [given[pl.ds(t * 8 + 6, PENCIL, stride=16), :] for t in range(2)]
    for i in range(8):
        value = turn(rest[i // 4], 64 - 32 * (i % 4)) if i < FIRSTS else jnp.zeros((PENCIL, 128), jnp.float32)
        third[pl.ds(i, PENCIL, stride=8), :] = value
    lane = lanes(8, 128)
    for p in range(PENCIL):
        parts = [given[p * 16 : p * 16 + 8, :], given[p * 16 + 8 : p * 16 + 16, :]]
        last = jnp.where(lane < 64, turn(parts[1], 64), third[p * 8 : p * 8 + 8, :])
        parts.append(jnp.where(lane < 32, turn(parts[0], 32), last))
        for u in range(2 * NB):
            for t in range(THIRDS):
                at = u * 24 + t * 8
                lines[at : at + 8, p * COLS : p * COLS + COLS] = parts[t][:, u * COLS : u * COLS + COLS]
    spectrum = dot(lines[...], forward[...])
    row = lax.broadcasted_iota(jnp.int32, (24, 128), 0)
    lane = lanes(24, 128)
    third_mode = THIRDS * lax.axis_index("slab") + row // 8
    first_mode = FIRSTS * lax.axis_index("pencil") + row % 8
    known = (row % 8 < FIRSTS) & (lane < MODES)
    squared = jnp.zeros((24, 128), jnp.int32)
    weight = jnp.full((24, 128), 1.0 / CELLS, jnp.float32)
    for mode in (third_mode, first_mode, lane):
        size = jnp.where(mode < CUT, mode, mode - CUT)
        squared = squared + size * size
        weight = weight * jnp.where(mode == 0, 1.0, jnp.where(mode == CUT, 0.0, 2.0))
    kinetic = squared.astype(jnp.float32) * (4.0 / CUT**2)
    kinetic = jnp.where(known & (squared < CUT * CUT), kinetic, 0.0)
    weight = weight * kinetic
    scaled, other = [], []
    for b in range(NB):
        alpha = jnp.where(flags[b] == 1, 1.0 / 1.5, 0.0)
        value = spectrum[b * 24 : b * 24 + 24] * alpha
        scaled.append(value * weight)
        other.append(0.5 * kinetic * value + spectrum[(NB + b) * 24 : (NB + b) * 24 + 24])
    returned = dot(jnp.concatenate(scaled, axis=0), back[...])
    rows[...] = jnp.zeros_like(rows)
    for q, (a, b) in enumerate(PAIRS):
        term = scaled[a] * other[b] + scaled[b] * other[a]
        rows[q : q + 1, :] = jnp.sum(term[:8] + term[8:16] + term[16:], axis=0, keepdims=True)
    total = jnp.sum(rows[...], axis=1, keepdims=True) + jnp.sum(sums[...], axis=1, keepdims=True)
    picked = lax.broadcasted_iota(jnp.int32, (16, 128), 0) == lanes(16, 128)
    note = jnp.sum(jnp.where(picked, total, 0.0), axis=0, keepdims=True)
    for p in range(PENCIL):
        for b in range(NB):
            for t in range(THIRDS):
                at = t * HALF + b * COLS
                wide[p * 8 : p * 8 + 8, at : at + COLS] = returned[b * 24 + t * 8 : b * 24 + t * 8 + 8, p * COLS : p * COLS + COLS]
    more[...] = wide[:, 128:256]
    out[...] = wide[:, 0:128]
    pieces = [more[pl.ds(i, PENCIL, stride=8), :] for i in range(FIRSTS)]
    out[pl.ds(6, PENCIL, stride=8), :] = gathered(pieces, 16, 0)
    out[pl.ds(7, PENCIL, stride=8), :] = jnp.broadcast_to(note, (PENCIL, 128))


def back_first(given, table, out, taken, made):
    rest = given[pl.ds(6, PENCIL, stride=8), :]
    for i in range(8):
        value = turn(rest, -16 * i) if i < FIRSTS else jnp.zeros((PENCIL, 128), jnp.float32)
        taken[pl.ds(i, PENCIL, stride=8), :] = value
    out[...] = dot(table[...], given[...])
    made[...] = dot(table[...], taken[...])
    pieces = [made[pl.ds(i, SLAB, stride=8), :] for i in range(ROWS)]
    out[pl.ds(6, SLAB, stride=8), :] = gathered(pieces, 16, 0)
    note = jnp.sum(given[pl.ds(7, PENCIL, stride=8), :], axis=0, keepdims=True)
    out[pl.ds(7, SLAB, stride=8), :] = jnp.broadcast_to(note, (SLAB, 128))


def back_third(given, local, table, out, lines):
    rest = given[pl.ds(6, SLAB, stride=8), :]
    for i in range(ROWS):
        value = given[pl.ds(i, SLAB, stride=8), :]
        at = i * HALF
        lines[0:32, at : at + HALF] = value[:, :HALF]
        lines[32:64, at : at + HALF] = value[:, HALF:WIDE]
        lines[64:96, at : at + 32] = value[:, WIDE:128]
        lines[64:96, at + 32 : at + HALF] = rest[:, 16 * i : 16 * i + 16]
    kinetic_part = dot(lines[...], table[...], ((0,), (0,)))
    note = jnp.sum(given[pl.ds(7, SLAB, stride=8), :], axis=0, keepdims=True) * (1.0 / CELLS)
    factor, inverse = {}, {}
    for q, (a, b) in enumerate(PAIRS):
        value = note[:, q : q + 1]
        for c in range(b):
            value = value - factor[a, c] * factor[b, c]
        if a == b:
            factor[a, a] = jnp.sqrt(value)
            inverse[a] = 1.0 / factor[a, a]
        else:
            factor[a, b] = value * inverse[b]
    for i in range(ROWS):
        done = []
        for a in range(NB):
            value = local[a, i] + kinetic_part[i * HALF + a * COLS : i * HALF + a * COLS + COLS]
            for b in range(a):
                value = value - factor[a, b] * done[b]
            value = value * inverse[a]
            done.append(value)
            out[i, :, a, :] = value


def smem():
    return pl.BlockSpec(memory_space=pltpu.SMEM)


def vmem():
    return pl.BlockSpec(memory_space=pltpu.VMEM)


def held(*shape):
    return pltpu.VMEM(shape, jnp.float32)


def f32(*shape):
    return jax.ShapeDtypeStruct(shape, jnp.float32)


def call(body, kinds, outs, scratch=()):
    made = pl.pallas_call(
        body,
        out_shape=outs,
        in_specs=[smem() if kind == "s" else vmem() for kind in kinds],
        out_specs=jax.tree.map(lambda _: vmem(), outs),
        scratch_shapes=[pltpu.VMEM(shape, jnp.float32) for shape in scratch],
        name=body.__name__,
    )

    def run(*given):
        kept = [pltpu.with_memory_space_constraint(x, pltpu.VMEM) if kind == "k" else x for kind, x in zip(kinds, given)]
        return made(*kept)

    return run


def trade(value, axis, number):
    blocks = value.reshape(number, -1, 128)
    return lax.all_to_all(blocks, axis, split_axis=0, concat_axis=0, tiled=True).reshape(value.shape)


def local_step(orbitals, potential, unlocked):
    third, first, first_back, second, second_back = tables()
    outs = (held(SLAB * 16, 128), held(NB, ROWS, COLS, NG), held(16, NG))
    made = call(forward_third, "svvv", outs, [(ROWS * 128, NG)])
    spectrum, local, sums = made(unlocked, orbitals.transpose(1, 2, 0, 3), potential, third)
    spectrum = trade(spectrum, "slab", SLAB)
    made = call(forward_first, "kv", held(PENCIL * 16, 128), [(SLAB * 8, 128), (PENCIL * 8, 128)])
    spectrum = trade(made(spectrum, first), "pencil", PENCIL)
    scratch = [(PENCIL * 8, 128), (8 * 24, NG), (PENCIL * 8, 256), (PENCIL * 8, 128), (16, 128)]
    made = call(middle, "skkvv", held(PENCIL * 8, 128), scratch)
    spectrum = trade(made(unlocked, spectrum, sums, second, second_back), "pencil", PENCIL)
    made = call(back_first, "kv", held(SLAB * 8, 128), [(PENCIL * 8, 128), (SLAB * 8, 128)])
    spectrum = trade(made(spectrum, first_back), "slab", SLAB)
    made = call(back_third, "kkv", f32(ROWS, COLS, NB, NG), [(MODES, ROWS * HALF)])
    return made(spectrum, local, third).transpose(2, 0, 1, 3)


def solution(mesh):
    in_specs = (P(None, "slab", "pencil", None), P("slab", "pencil", None), P())
    out_specs = P(None, "slab", "pencil", None)
    return jax.shard_map(local_step, mesh=mesh, in_specs=in_specs, out_specs=out_specs, check_vma=False)
```

```python
import functools

import jax
import jax.numpy as jnp
import numpy as np
from jax import lax
from jax.experimental import pallas as pl
from jax.experimental.pallas import tpu as pltpu
from jax.sharding import PartitionSpec as P

NG = 192
NB = 4
CUT = NG // 4
MODES = 2 * CUT
SLAB = 32
PENCIL = 16
ROWS = NG // SLAB
COLS = NG // PENCIL
CELLS = float(NG**3)
THIRDS = MODES // SLAB
FIRSTS = MODES // PENCIL
WIDE = 2 * NB * COLS
HALF = NB * COLS
PAIRS = [(a, b) for a in range(NB) for b in range(a + 1)]
highest = lax.Precision.HIGHEST


def basis():
    place = np.arange(NG)
    mode = np.arange(MODES)
    angle = 2.0 * np.pi / NG * ((mode[:, None] % CUT) * place[None, :] % NG)
    return np.where(mode[:, None] < CUT, np.cos(angle), np.sin(angle))


def tables():
    real = basis()
    third = real.reshape(SLAB, THIRDS, NG).transpose(1, 0, 2).reshape(MODES, NG)
    first = np.zeros((PENCIL, 8, SLAB, 8))
    first[:, :FIRSTS, :, :ROWS] = real.reshape(PENCIL, FIRSTS, SLAB, ROWS)
    first = first.reshape(PENCIL * 8, SLAB * 8)
    second = np.zeros((128, NG))
    second[:MODES] = real
    made = (third, first, first.T, second.T, second)
    return [np.ascontiguousarray(t, dtype=np.float32) for t in made]


def dot(a, b, dims=((1,), (0,))):
    return lax.dot_general(a, b, (dims, ((), ())), precision=highest, preferred_element_type=jnp.float32)


def lanes(*shape):
    return lax.broadcasted_iota(jnp.int32, shape, len(shape) - 1)


def turn(value, by):
    by = by % 128
    return pltpu.roll(value, by, 1) if by else value


def gathered(pieces, width, start):
    lane = lanes(*pieces[0].shape)
    result = jnp.zeros(pieces[0].shape, jnp.float32)
    for k, piece in enumerate(pieces):
        here = (lane >= k * width) & (lane < k * width + width)
        result = jnp.where(here, turn(piece, k * width - start), result)
    return result


def forward_third(flags, orbitals, potential, table, out, local, sums, lines):
    totals = [None] * len(PAIRS)
    for i in range(ROWS):
        shifted = (potential[i] - 1.0) * (1.0 / 1.5)
        own = []
        for b in range(NB):
            base = i * 128 + b * COLS
            value = orbitals[i, :, b, :]
            kept = jnp.where(flags[b] == 1, value * shifted, value)
            lines[base : base + COLS, :] = value
            lines[base + HALF : base + HALF + COLS, :] = kept
            local[b, i] = kept
            own.append(kept)
        for q, (a, b) in enumerate(PAIRS):
            term = own[a] * own[b]
            totals[q] = term if totals[q] is None else totals[q] + term
    sums[...] = jnp.zeros_like(sums)
    for q in range(len(PAIRS)):
        sums[q : q + 1, :] = jnp.sum(totals[q], axis=0, keepdims=True)
    spectrum = dot(table[...], lines[...], ((1,), (1,)))
    whole = lanes(SLAB, 128)
    last = []
    for i in range(ROWS):
        parts = [spectrum[t * 32 : t * 32 + 32, i * 128 : i * 128 + 128] for t in range(THIRDS)]
        for t in range(2):
            extra = turn(parts[2], WIDE - 32 * t)
            out[pl.ds(t * 8 + i, SLAB, stride=16), :] = jnp.where(whole < WIDE, parts[t], extra)
        last.append(parts[2])
    for t in range(2):
        out[pl.ds(t * 8 + 6, SLAB, stride=16), :] = gathered(last[t * 4 : t * 4 + 4], 32, 64)
        out[pl.ds(t * 8 + 7, SLAB, stride=16), :] = jnp.zeros((SLAB, 128), jnp.float32)


def forward_first(given, table, out, taken, made):
    rest = [given[pl.ds(t * 8 + 6, SLAB, stride=16), :] for t in range(2)]
    for i in range(8):
        value = turn(rest[i // 4], -32 * (i % 4)) if i < ROWS else jnp.zeros((SLAB, 128), jnp.float32)
        taken[pl.ds(i, SLAB, stride=8), :] = value
    tiles = given[...].reshape(SLAB, 16, 128)
    for t in range(2):
        block = tiles[:, t * 8 : t * 8 + 8].reshape(SLAB * 8, 128)
        result = dot(table[...], block)
        for p in range(PENCIL):
            out[p * 16 + t * 8 : p * 16 + t * 8 + 8, :] = result[p * 8 : p * 8 + 8]
    made[...] = dot(table[...], taken[...])
    pieces = [made[pl.ds(i, PENCIL, stride=8), :] for i in range(FIRSTS)]
    for t in range(2):
        out[pl.ds(t * 8 + 6, PENCIL, stride=16), :] = gathered(pieces[t * 4 : t * 4 + 4], 32, 0)


def middle(flags, given, sums, forward, back, out, third, lines, wide, more, rows):
    rest = [given[pl.ds(t * 8 + 6, PENCIL, stride=16), :] for t in range(2)]
    for i in range(8):
        value = turn(rest[i // 4], 64 - 32 * (i % 4)) if i < FIRSTS else jnp.zeros((PENCIL, 128), jnp.float32)
        third[pl.ds(i, PENCIL, stride=8), :] = value
    lane = lanes(8, 128)
    for p in range(PENCIL):
        parts = [given[p * 16 : p * 16 + 8, :], given[p * 16 + 8 : p * 16 + 16, :]]
        last = jnp.where(lane < 64, turn(parts[1], 64), third[p * 8 : p * 8 + 8, :])
        parts.append(jnp.where(lane < 32, turn(parts[0], 32), last))
        for u in range(2 * NB):
            for t in range(THIRDS):
                at = u * 24 + t * 8
                lines[at : at + 8, p * COLS : p * COLS + COLS] = parts[t][:, u * COLS : u * COLS + COLS]
    spectrum = dot(lines[...], forward[...])
    row = lax.broadcasted_iota(jnp.int32, (24, 128), 0)
    lane = lanes(24, 128)
    third_mode = THIRDS * lax.axis_index("slab") + row // 8
    first_mode = FIRSTS * lax.axis_index("pencil") + row % 8
    known = (row % 8 < FIRSTS) & (lane < MODES)
    squared = jnp.zeros((24, 128), jnp.int32)
    weight = jnp.full((24, 128), 1.0 / CELLS, jnp.float32)
    for mode in (third_mode, first_mode, lane):
        size = jnp.where(mode < CUT, mode, mode - CUT)
        squared = squared + size * size
        weight = weight * jnp.where(mode == 0, 1.0, jnp.where(mode == CUT, 0.0, 2.0))
    kinetic = squared.astype(jnp.float32) * (4.0 / CUT**2)
    kinetic = jnp.where(known & (squared < CUT * CUT), kinetic, 0.0)
    weight = weight * kinetic
    scaled, other = [], []
    for b in range(NB):
        alpha = jnp.where(flags[b] == 1, 1.0 / 1.5, 0.0)
        value = spectrum[b * 24 : b * 24 + 24] * alpha
        scaled.append(value * weight)
        other.append(0.5 * kinetic * value + spectrum[(NB + b) * 24 : (NB + b) * 24 + 24])
    returned = dot(jnp.concatenate(scaled, axis=0), back[...])
    rows[...] = jnp.zeros_like(rows)
    for q, (a, b) in enumerate(PAIRS):
        term = scaled[a] * other[b] + scaled[b] * other[a]
        rows[q : q + 1, :] = jnp.sum(term[:8] + term[8:16] + term[16:], axis=0, keepdims=True)
    total = jnp.sum(rows[...], axis=1, keepdims=True) + jnp.sum(sums[...], axis=1, keepdims=True)
    picked = lax.broadcasted_iota(jnp.int32, (16, 128), 0) == lanes(16, 128)
    note = jnp.sum(jnp.where(picked, total, 0.0), axis=0, keepdims=True)
    for p in range(PENCIL):
        for b in range(NB):
            for t in range(THIRDS):
                at = t * HALF + b * COLS
                wide[p * 8 : p * 8 + 8, at : at + COLS] = returned[b * 24 + t * 8 : b * 24 + t * 8 + 8, p * COLS : p * COLS + COLS]
    more[...] = wide[:, 128:256]
    out[...] = wide[:, 0:128]
    pieces = [more[pl.ds(i, PENCIL, stride=8), :] for i in range(FIRSTS)]
    out[pl.ds(6, PENCIL, stride=8), :] = gathered(pieces, 16, 0)
    out[pl.ds(7, PENCIL, stride=8), :] = jnp.broadcast_to(note, (PENCIL, 128))


def back_first(given, table, out, taken, made):
    rest = given[pl.ds(6, PENCIL, stride=8), :]
    for i in range(8):
        value = turn(rest, -16 * i) if i < FIRSTS else jnp.zeros((PENCIL, 128), jnp.float32)
        taken[pl.ds(i, PENCIL, stride=8), :] = value
    out[...] = dot(table[...], given[...])
    made[...] = dot(table[...], taken[...])
    pieces = [made[pl.ds(i, SLAB, stride=8), :] for i in range(ROWS)]
    out[pl.ds(6, SLAB, stride=8), :] = gathered(pieces, 16, 0)
    note = jnp.sum(given[pl.ds(7, PENCIL, stride=8), :], axis=0, keepdims=True)
    out[pl.ds(7, SLAB, stride=8), :] = jnp.broadcast_to(note, (SLAB, 128))


def back_third(given, local, table, out, lines):
    rest = given[pl.ds(6, SLAB, stride=8), :]
    for i in range(ROWS):
        value = given[pl.ds(i, SLAB, stride=8), :]
        at = i * HALF
        lines[0:32, at : at + HALF] = value[:, :HALF]
        lines[32:64, at : at + HALF] = value[:, HALF:WIDE]
        lines[64:96, at : at + 32] = value[:, WIDE:128]
        lines[64:96, at + 32 : at + HALF] = rest[:, 16 * i : 16 * i + 16]
    kinetic_part = dot(lines[...], table[...], ((0,), (0,)))
    note = jnp.sum(given[pl.ds(7, SLAB, stride=8), :], axis=0, keepdims=True) * (1.0 / CELLS)
    factor, inverse = {}, {}
    for q, (a, b) in enumerate(PAIRS):
        value = note[:, q : q + 1]
        for c in range(b):
            value = value - factor[a, c] * factor[b, c]
        if a == b:
            factor[a, a] = jnp.sqrt(value)
            inverse[a] = 1.0 / factor[a, a]
        else:
            factor[a, b] = value * inverse[b]
    for i in range(ROWS):
        done = []
        for a in range(NB):
            value = local[a, i] + kinetic_part[i * HALF + a * COLS : i * HALF + a * COLS + COLS]
            for b in range(a):
                value = value - factor[a, b] * done[b]
            value = value * inverse[a]
            done.append(value)
            out[i, :, a, :] = value


def smem():
    return pl.BlockSpec(memory_space=pltpu.SMEM)


def vmem():
    return pl.BlockSpec(memory_space=pltpu.VMEM)


def held(*shape):
    return pltpu.VMEM(shape, jnp.float32)


def f32(*shape):
    return jax.ShapeDtypeStruct(shape, jnp.float32)


def call(body, kinds, outs, scratch=()):
    made = pl.pallas_call(
        body,
        out_shape=outs,
        in_specs=[smem() if kind == "s" else vmem() for kind in kinds],
        out_specs=jax.tree.map(lambda _: vmem(), outs),
        scratch_shapes=[pltpu.VMEM(shape, jnp.float32) for shape in scratch],
        name=body.__name__,
    )

    def run(*given):
        kept = [pltpu.with_memory_space_constraint(x, pltpu.VMEM) if kind == "k" else x for kind, x in zip(kinds, given)]
        return made(*kept)

    return run


def trade(value, axis, number):
    blocks = value.reshape(number, -1, 128)
    return lax.all_to_all(blocks, axis, split_axis=0, concat_axis=0, tiled=True).reshape(value.shape)


def local_step(orbitals, potential, unlocked):
    third, first, first_back, second, second_back = tables()
    outs = (held(SLAB * 16, 128), held(NB, ROWS, COLS, NG), held(16, NG))
    made = call(forward_third, "svvv", outs, [(ROWS * 128, NG)])
    spectrum, local, sums = made(unlocked, orbitals.transpose(1, 2, 0, 3), potential, third)
    spectrum = trade(spectrum, "slab", SLAB)
    made = call(forward_first, "kk", held(PENCIL * 16, 128), [(SLAB * 8, 128), (PENCIL * 8, 128)])
    spectrum = trade(made(spectrum, first), "pencil", PENCIL)
    scratch = [(PENCIL * 8, 128), (8 * 24, NG), (PENCIL * 8, 256), (PENCIL * 8, 128), (16, 128)]
    made = call(middle, "skkkk", held(PENCIL * 8, 128), scratch)
    spectrum = trade(made(unlocked, spectrum, sums, second, second_back), "pencil", PENCIL)
    made = call(back_first, "kk", held(SLAB * 8, 128), [(PENCIL * 8, 128), (SLAB * 8, 128)])
    spectrum = trade(made(spectrum, first_back), "slab", SLAB)
    made = call(back_third, "kkk", f32(ROWS, COLS, NB, NG), [(MODES, ROWS * HALF)])
    return made(spectrum, local, third).transpose(2, 0, 1, 3)


def solution(mesh):
    in_specs = (P(None, "slab", "pencil", None), P("slab", "pencil", None), P())
    out_specs = P(None, "slab", "pencil", None)
    return jax.shard_map(local_step, mesh=mesh, in_specs=in_specs, out_specs=out_specs, check_vma=False)
```

```python
import functools

import jax
import jax.numpy as jnp
import numpy as np
from jax import lax
from jax.experimental import pallas as pl
from jax.experimental.pallas import tpu as pltpu
from jax.sharding import PartitionSpec as P

NG = 192
NB = 4
CUT = NG // 4
MODES = 2 * CUT
SLAB = 32
PENCIL = 16
ROWS = NG // SLAB
COLS = NG // PENCIL
CELLS = float(NG**3)
THIRDS = MODES // SLAB
FIRSTS = MODES // PENCIL
WIDE = 2 * NB * COLS
HALF = NB * COLS
PAIRS = [(a, b) for a in range(NB) for b in range(a + 1)]
highest = lax.Precision.HIGHEST


def basis():
    place = np.arange(NG)
    mode = np.arange(MODES)
    angle = 2.0 * np.pi / NG * ((mode[:, None] % CUT) * place[None, :] % NG)
    return np.where(mode[:, None] < CUT, np.cos(angle), np.sin(angle))


def tables():
    real = basis()
    third = real.reshape(SLAB, THIRDS, NG).transpose(1, 0, 2).reshape(MODES, NG)
    first = np.zeros((PENCIL, 8, SLAB, 8))
    first[:, :FIRSTS, :, :ROWS] = real.reshape(PENCIL, FIRSTS, SLAB, ROWS)
    first = first.reshape(PENCIL * 8, SLAB * 8)
    second = np.zeros((128, 2, 128))
    second[:MODES, :, : NG // 2] = real.reshape(MODES, 2, NG // 2)
    second = second.reshape(128, 256)
    made = (third, first, first.T, second.T, second)
    return [np.ascontiguousarray(t, dtype=np.float32) for t in made]


def dot(a, b, dims=((1,), (0,))):
    return lax.dot_general(a, b, (dims, ((), ())), precision=highest, preferred_element_type=jnp.float32)


def lanes(*shape):
    return lax.broadcasted_iota(jnp.int32, shape, len(shape) - 1)


def turn(value, by):
    by = by % 128
    return pltpu.roll(value, by, 1) if by else value


def gathered(pieces, width, start):
    lane = lanes(*pieces[0].shape)
    result = jnp.zeros(pieces[0].shape, jnp.float32)
    for k, piece in enumerate(pieces):
        here = (lane >= k * width) & (lane < k * width + width)
        result = jnp.where(here, turn(piece, k * width - start), result)
    return result


def forward_third(flags, orbitals, potential, table, out, local, sums, lines):
    totals = [None] * len(PAIRS)
    whole = lanes(SLAB, 128)
    last = []
    for i in range(ROWS):
        shifted = (potential[i] - 1.0) * (1.0 / 1.5)
        own = []
        for b in range(NB):
            base = i * 128 + b * COLS
            value = orbitals[i, :, b, :]
            kept = jnp.where(flags[b] == 1, value * shifted, value)
            lines[base : base + COLS, :] = value * jnp.where(flags[b] == 1, 1.0 / 1.5, 0.0)
            lines[base + HALF : base + HALF + COLS, :] = kept
            local[b, i] = kept
            own.append(kept)
        for q, (a, b) in enumerate(PAIRS):
            term = own[a] * own[b]
            totals[q] = term if totals[q] is None else totals[q] + term
    sums[...] = jnp.zeros_like(sums)
    for q in range(len(PAIRS)):
        sums[q : q + 1, :] = jnp.sum(totals[q], axis=0, keepdims=True)
    for pair in range(ROWS // 2):
        spectrum = dot(table[...], lines[pair * 256 : pair * 256 + 256, :], ((1,), (1,)))
        for i in (2 * pair, 2 * pair + 1):
            at = i % 2 * 128
            parts = [spectrum[t * 32 : t * 32 + 32, at : at + 128] for t in range(THIRDS)]
            for t in range(2):
                extra = turn(parts[2], WIDE - 32 * t)
                out[pl.ds(t * 8 + i, SLAB, stride=16), :] = jnp.where(whole < WIDE, parts[t], extra)
            last.append(parts[2])
    for t in range(2):
        out[pl.ds(t * 8 + 6, SLAB, stride=16), :] = gathered(last[t * 4 : t * 4 + 4], 32, 64)
        out[pl.ds(t * 8 + 7, SLAB, stride=16), :] = jnp.zeros((SLAB, 128), jnp.float32)


def forward_first(given, table, out, taken, made):
    rest = [given[pl.ds(t * 8 + 6, SLAB, stride=16), :] for t in range(2)]
    for i in range(8):
        value = turn(rest[i // 4], -32 * (i % 4)) if i < ROWS else jnp.zeros((SLAB, 128), jnp.float32)
        taken[pl.ds(i, SLAB, stride=8), :] = value
    tiles = given[...].reshape(SLAB, 16, 128)
    for t in range(2):
        block = tiles[:, t * 8 : t * 8 + 8].reshape(SLAB * 8, 128)
        result = dot(table[...], block)
        for p in range(PENCIL):
            out[p * 16 + t * 8 : p * 16 + t * 8 + 8, :] = result[p * 8 : p * 8 + 8]
    made[...] = dot(table[...], taken[...])
    pieces = [made[pl.ds(i, PENCIL, stride=8), :] for i in range(FIRSTS)]
    for t in range(2):
        out[pl.ds(t * 8 + 6, PENCIL, stride=16), :] = gathered(pieces[t * 4 : t * 4 + 4], 32, 0)


def middle(given, sums, forward, back, out, third, lines, more, rows):
    rest = [given[pl.ds(t * 8 + 6, PENCIL, stride=16), :] for t in range(2)]
    for i in range(8):
        value = turn(rest[i // 4], 64 - 32 * (i % 4)) if i < FIRSTS else jnp.zeros((PENCIL, 128), jnp.float32)
        third[pl.ds(i, PENCIL, stride=8), :] = value
    lane = lanes(8, 128)
    masks = [((lane - COLS * m) & 127) < COLS for m in range(17)]
    for h in range(2):
        turned = [[], [], []]
        for k in range(8):
            p = 8 * h + k
            parts = [given[p * 16 : p * 16 + 8, :], given[p * 16 + 8 : p * 16 + 16, :]]
            last = jnp.where(lane < 64, turn(parts[1], 64), third[p * 8 : p * 8 + 8, :])
            parts.append(jnp.where(lane < 32, turn(parts[0], 32), last))
            for t in range(THIRDS):
                turned[t].append(turn(parts[t], COLS * k))
        for t in range(THIRDS):
            for u in range(2 * NB):
                value = turned[t][0]
                for k in range(1, 8):
                    value = jnp.where(masks[k + u], turned[t][k], value)
                lines[u * 24 + t * 8 : u * 24 + t * 8 + 8, h * 128 : h * 128 + 128] = turn(value, -COLS * u)
    spectrum = dot(lines[...], forward[...])
    row = lax.broadcasted_iota(jnp.int32, (24, 128), 0)
    lane = lanes(24, 128)
    third_mode = THIRDS * lax.axis_index("slab") + row // 8
    first_mode = FIRSTS * lax.axis_index("pencil") + row % 8
    known = (row % 8 < FIRSTS) & (lane < MODES)
    squared = jnp.zeros((24, 128), jnp.int32)
    weight = jnp.full((24, 128), 1.0 / CELLS, jnp.float32)
    for mode in (third_mode, first_mode, lane):
        size = jnp.where(mode < CUT, mode, mode - CUT)
        squared = squared + size * size
        weight = weight * jnp.where(mode == 0, 1.0, jnp.where(mode == CUT, 0.0, 2.0))
    kinetic = squared.astype(jnp.float32) * (4.0 / CUT**2)
    kinetic = jnp.where(known & (squared < CUT * CUT), kinetic, 0.0)
    weight = weight * kinetic
    scaled, other = [], []
    for b in range(NB):
        value = spectrum[b * 24 : b * 24 + 24]
        scaled.append(value * weight)
        other.append(0.5 * kinetic * value + spectrum[(NB + b) * 24 : (NB + b) * 24 + 24])
    returned = dot(jnp.concatenate(scaled, axis=0), back[...])
    rows[...] = jnp.zeros_like(rows)
    for q, (a, b) in enumerate(PAIRS):
        term = scaled[a] * other[b] + scaled[b] * other[a]
        rows[q : q + 1, :] = jnp.sum(term[:8] + term[8:16] + term[16:], axis=0, keepdims=True)
    total = jnp.sum(rows[...], axis=1, keepdims=True) + jnp.sum(sums[...], axis=1, keepdims=True)
    picked = lax.broadcasted_iota(jnp.int32, (16, 128), 0) + 64 == lanes(16, 128)
    note = jnp.sum(jnp.where(picked, total, 0.0), axis=0, keepdims=True)
    for h in range(2):
        turned = []
        for c in range(NB * THIRDS):
            t, b = c // NB, c % NB
            value = returned[b * 24 + t * 8 : b * 24 + t * 8 + 8, h * 128 : h * 128 + 128]
            turned.append(turn(value, COLS * (c if c < 10 else c - 10)))
        for k in range(8):
            p = 8 * h + k
            value = turned[0]
            for c in range(1, 10):
                value = jnp.where(masks[k + c], turned[c], value)
            out[p * 8 : p * 8 + 8, :] = turn(value, -COLS * k)
            more[p * 8 : p * 8 + 8, :] = turn(jnp.where(masks[k + 1], turned[11], turned[10]), -COLS * k)
    pieces = [more[pl.ds(i, PENCIL, stride=8), :] for i in range(FIRSTS)]
    out[pl.ds(6, PENCIL, stride=8), :] = gathered(pieces[:5], 24, 0)
    out[pl.ds(7, PENCIL, stride=8), :] = jnp.where(lanes(PENCIL, 128) < 24, pieces[5], note)


def back_first(given, table, out, taken, made):
    rest = [given[pl.ds(i, PENCIL, stride=8), :] for i in (6, 7)]
    for i in range(8):
        value = turn(rest[i // 5], -24 * (i % 5)) if i < FIRSTS else jnp.zeros((PENCIL, 128), jnp.float32)
        taken[pl.ds(i, PENCIL, stride=8), :] = value
    out[...] = dot(table[...], given[...])
    made[...] = dot(table[...], taken[...])
    pieces = [made[pl.ds(i, SLAB, stride=8), :] for i in range(ROWS)]
    out[pl.ds(6, SLAB, stride=8), :] = gathered(pieces[:5], 24, 0)
    note = jnp.sum(rest[1], axis=0, keepdims=True)
    out[pl.ds(7, SLAB, stride=8), :] = jnp.where(lanes(SLAB, 128) < 24, pieces[5], note)


def back_third(given, local, table, out, lines):
    rest = [given[pl.ds(i, SLAB, stride=8), :] for i in (6, 7)]
    for i in range(ROWS):
        value = given[pl.ds(i, SLAB, stride=8), :]
        at = i * HALF
        lines[0:32, at : at + HALF] = value[:, :HALF]
        lines[32:64, at : at + HALF] = value[:, HALF:WIDE]
        lines[64:96, at : at + 24] = value[:, WIDE : WIDE + 24]
        lines[64:96, at + 24 : at + HALF] = rest[i // 5][:, 24 * (i % 5) : 24 * (i % 5) + 24]
    kinetic_part = dot(lines[...], table[...], ((0,), (0,)))
    note = jnp.sum(rest[1], axis=0, keepdims=True) * (1.0 / CELLS)
    factor, inverse = {}, {}
    for q, (a, b) in enumerate(PAIRS):
        value = note[:, 64 + q : 65 + q]
        for c in range(b):
            value = value - factor[a, c] * factor[b, c]
        if a == b:
            factor[a, a] = jnp.sqrt(value)
            inverse[a] = 1.0 / factor[a, a]
        else:
            factor[a, b] = value * inverse[b]
    for i in range(ROWS):
        done = []
        for a in range(NB):
            value = local[a, i] + kinetic_part[i * HALF + a * COLS : i * HALF + a * COLS + COLS]
            for b in range(a):
                value = value - factor[a, b] * done[b]
            value = value * inverse[a]
            done.append(value)
            out[i, :, a, :] = value


def smem():
    return pl.BlockSpec(memory_space=pltpu.SMEM)


def vmem():
    return pl.BlockSpec(memory_space=pltpu.VMEM)


def held(*shape):
    return pltpu.VMEM(shape, jnp.float32)


def f32(*shape):
    return jax.ShapeDtypeStruct(shape, jnp.float32)


def call(body, kinds, outs, scratch=()):
    made = pl.pallas_call(
        body,
        out_shape=outs,
        in_specs=[smem() if kind == "s" else vmem() for kind in kinds],
        out_specs=jax.tree.map(lambda _: vmem(), outs),
        scratch_shapes=[pltpu.VMEM(shape, jnp.float32) for shape in scratch],
        name=body.__name__,
    )

    def run(*given):
        kept = [pltpu.with_memory_space_constraint(x, pltpu.VMEM) if kind == "k" else x for kind, x in zip(kinds, given)]
        return made(*kept)

    return run


def trade(value, axis, number):
    blocks = value.reshape(number, -1, 128)
    return lax.all_to_all(blocks, axis, split_axis=0, concat_axis=0, tiled=True).reshape(value.shape)


def local_step(orbitals, potential, unlocked):
    third, first, first_back, second, second_back = tables()
    outs = (held(SLAB * 16, 128), held(NB, ROWS, COLS, NG), held(16, NG))
    made = call(forward_third, "svvv", outs, [(ROWS * 128, NG)])
    spectrum, local, sums = made(unlocked, orbitals.transpose(1, 2, 0, 3), potential, third)
    spectrum = trade(spectrum, "slab", SLAB)
    made = call(forward_first, "kk", held(PENCIL * 16, 128), [(SLAB * 8, 128), (PENCIL * 8, 128)])
    spectrum = trade(made(spectrum, first), "pencil", PENCIL)
    scratch = [(PENCIL * 8, 128), (8 * 24, 256), (PENCIL * 8, 128), (16, 128)]
    made = call(middle, "kkkk", held(PENCIL * 8, 128), scratch)
    spectrum = trade(made(spectrum, sums, second, second_back), "pencil", PENCIL)
    made = call(back_first, "kk", held(SLAB * 8, 128), [(PENCIL * 8, 128), (SLAB * 8, 128)])
    spectrum = trade(made(spectrum, first_back), "slab", SLAB)
    made = call(back_third, "kkk", f32(ROWS, COLS, NB, NG), [(MODES, ROWS * HALF)])
    return made(spectrum, local, third).transpose(2, 0, 1, 3)


def solution(mesh):
    in_specs = (P(None, "slab", "pencil", None), P("slab", "pencil", None), P())
    out_specs = P(None, "slab", "pencil", None)
    return jax.shard_map(local_step, mesh=mesh, in_specs=in_specs, out_specs=out_specs, check_vma=False)
```

```python
import functools

import jax
import jax.numpy as jnp
import numpy as np
from jax import lax
from jax.experimental import pallas as pl
from jax.experimental.pallas import tpu as pltpu
from jax.sharding import PartitionSpec as P

NG = 192
NB = 4
CUT = NG // 4
MODES = 2 * CUT
SLAB = 32
PENCIL = 16
ROWS = NG // SLAB
COLS = NG // PENCIL
CELLS = float(NG**3)
THIRDS = MODES // SLAB
FIRSTS = MODES // PENCIL
WIDE = 2 * NB * COLS
HALF = NB * COLS
PAIRS = [(a, b) for a in range(NB) for b in range(a + 1)]
highest = lax.Precision.HIGHEST


def basis():
    place = np.arange(NG)
    mode = np.arange(MODES)
    angle = 2.0 * np.pi / NG * ((mode[:, None] % CUT) * place[None, :] % NG)
    return np.where(mode[:, None] < CUT, np.cos(angle), np.sin(angle))


def tables():
    real = basis()
    third = real.reshape(SLAB, THIRDS, NG).transpose(1, 0, 2).reshape(MODES, NG)
    first = real.reshape(PENCIL, FIRSTS, SLAB, ROWS).transpose(1, 0, 3, 2).reshape(MODES, NG)
    second = np.zeros((128, 2, 128))
    second[:MODES, :, : NG // 2] = real.reshape(MODES, 2, NG // 2)
    second = second.reshape(128, 256)
    made = (third, first, first.T, second.T, second)
    return [np.ascontiguousarray(t, dtype=np.float32) for t in made]


def dot(a, b, dims=((1,), (0,))):
    return lax.dot_general(a, b, (dims, ((), ())), precision=highest, preferred_element_type=jnp.float32)


def lanes(*shape):
    return lax.broadcasted_iota(jnp.int32, shape, len(shape) - 1)


def turn(value, by):
    by = by % 128
    return pltpu.roll(value, by, 1) if by else value


def gathered(pieces, width, start):
    lane = lanes(*pieces[0].shape)
    result = jnp.zeros(pieces[0].shape, jnp.float32)
    for k, piece in enumerate(pieces):
        here = (lane >= k * width) & (lane < k * width + width)
        result = jnp.where(here, turn(piece, k * width - start), result)
    return result


def forward_third(flags, orbitals, potential, table, out, local, sums, kind, low, high, field, made, lines, ready):
    copies = [pltpu.make_async_copy(flags, kind, ready.at[0]), pltpu.make_async_copy(potential, field, ready.at[1])]
    copies += [pltpu.make_async_copy(orbitals.at[i, :, :, 0:128], low.at[i], ready.at[2 + i]) for i in range(ROWS)]
    copies += [pltpu.make_async_copy(orbitals.at[i, :, :, 128:NG], high.at[i], ready.at[2 + ROWS + i]) for i in range(ROWS)]
    copies.append(pltpu.make_async_copy(table, made, ready.at[2 + 2 * ROWS]))
    low, high = low.reshape(ROWS * COLS * NB, 128), high.reshape(ROWS * COLS * NB, 64)
    for copy in copies:
        copy.start()
    copies[0].wait()
    copies[1].wait()
    totals = [None] * len(PAIRS)
    for i in range(ROWS):
        copies[2 + i].wait()
        copies[2 + ROWS + i].wait()
        shifted = (field[i] - 1.0) * (1.0 / 1.5)
        own = []
        for b in range(NB):
            base = i * WIDE + b * COLS
            parts = [ref[pl.ds(i * WIDE // 2 + b, COLS, stride=NB), :] for ref in (low, high)]
            value = jnp.concatenate([parts[0], parts[1]], axis=1)
            kept = jnp.where(kind[b] == 1, value * shifted, value)
            lines[base : base + COLS, :] = value * jnp.where(kind[b] == 1, 1.0 / 1.5, 0.0)
            lines[base + HALF : base + HALF + COLS, :] = kept
            local[b, i] = kept
            own.append(kept)
        for q, (a, b) in enumerate(PAIRS):
            term = own[a] * own[b]
            totals[q] = term if totals[q] is None else totals[q] + term
    copies[-1].wait()
    whole = lanes(SLAB, 128)
    last = []
    for i in range(ROWS):
        if i % 2 == 0:
            spectrum = dot(made[...], lines[i * WIDE : i * WIDE + 2 * WIDE, :], ((1,), (1,)))
            result = spectrum[:, :128]
        else:
            more = jnp.concatenate([spectrum[:, 128:], jnp.zeros((MODES, 64), jnp.float32)], axis=1)
            result = jnp.where(lanes(MODES, 128) < 32, turn(spectrum[:, :128], 32), turn(more, 32))
        parts = [result[t * 32 : t * 32 + 32] for t in range(THIRDS)]
        for t in range(2):
            extra = turn(parts[2], WIDE - 32 * t)
            out[pl.ds(t * 7 + i, SLAB, stride=14), :] = jnp.where(whole < WIDE, parts[t], extra)
        last.append(parts[2])
    sums[...] = jnp.zeros_like(sums)
    for q in range(len(PAIRS)):
        sums[q : q + 1, :] = jnp.sum(totals[q], axis=0, keepdims=True)
    for t in range(2):
        out[pl.ds(t * 7 + 6, SLAB, stride=14), :] = gathered(last[t * 4 : t * 4 + 4], 32, 64)


def forward_first(given, table, out):
    for t in range(2):
        block = jnp.concatenate([given[pl.ds(t * 7 + i, SLAB, stride=14), :] for i in range(ROWS)], axis=0)
        result = dot(table[...], block)
        for i in range(FIRSTS):
            out[pl.ds(t * 7 + i, PENCIL, stride=14), :] = result[i * PENCIL : (i + 1) * PENCIL]
    rest = [given[pl.ds(t * 7 + 6, SLAB, stride=14), :] for t in range(2)]
    block = jnp.concatenate([turn(rest[i // 4], -32 * (i % 4)) for i in range(ROWS)], axis=0)
    result = dot(table[...], block)
    pieces = [result[i * PENCIL : (i + 1) * PENCIL] for i in range(FIRSTS)]
    for t in range(2):
        out[pl.ds(t * 7 + 6, PENCIL, stride=14), :] = gathered(pieces[t * 4 : t * 4 + 4], 32, 0)


def middle(given, sums, forward, back, out, tiles, lines, more, rows):
    rest = [given[pl.ds(t * 7 + 6, PENCIL, stride=14), :] for t in range(2)]
    lane = lanes(PENCIL, 128)
    empty = jnp.zeros((PENCIL, 128), jnp.float32)
    for i in range(8):
        parts = [empty] * THIRDS
        if i < FIRSTS:
            parts = [given[pl.ds(t * 7 + i, PENCIL, stride=14), :] for t in range(2)]
            last = jnp.where(lane < 64, turn(parts[1], 64), turn(rest[i // 4], 64 - 32 * (i % 4)))
            parts.append(jnp.where(lane < 32, turn(parts[0], 32), last))
        for t in range(THIRDS):
            tiles[pl.ds(t * 128 + i, PENCIL, stride=8), :] = parts[t]
    lane = lanes(8, 128)
    masks = [((lane - COLS * m) & 127) < COLS for m in range(17)]
    for h in range(2):
        for t in range(THIRDS):
            turned = []
            for k in range(8):
                at = t * 128 + (8 * h + k) * 8
                turned.append(turn(tiles[at : at + 8, :], COLS * k))
            for u in range(2 * NB):
                value = turned[0]
                for k in range(1, 8):
                    value = jnp.where(masks[k + u], turned[k], value)
                lines[u * 24 + t * 8 : u * 24 + t * 8 + 8, h * 128 : h * 128 + 128] = turn(value, -COLS * u)
    spectrum = dot(lines[...], forward[...])
    row = lax.broadcasted_iota(jnp.int32, (24, 128), 0)
    lane = lanes(24, 128)
    third_mode = THIRDS * lax.axis_index("slab") + row // 8
    first_mode = FIRSTS * lax.axis_index("pencil") + row % 8
    known = (row % 8 < FIRSTS) & (lane < MODES)
    squared = jnp.zeros((24, 128), jnp.int32)
    weight = jnp.full((24, 128), 1.0 / CELLS, jnp.float32)
    for mode in (third_mode, first_mode, lane):
        size = jnp.where(mode < CUT, mode, mode - CUT)
        squared = squared + size * size
        weight = weight * jnp.where(mode == 0, 1.0, jnp.where(mode == CUT, 0.0, 2.0))
    kinetic = squared.astype(jnp.float32) * (4.0 / CUT**2)
    kinetic = jnp.where(known & (squared < CUT * CUT), kinetic, 0.0)
    weight = weight * kinetic
    scaled, other = [], []
    for b in range(NB):
        value = spectrum[b * 24 : b * 24 + 24]
        scaled.append(value * weight)
        other.append(0.5 * kinetic * value + spectrum[(NB + b) * 24 : (NB + b) * 24 + 24])
    returned = dot(jnp.concatenate(scaled, axis=0), back[...])
    rows[...] = jnp.zeros_like(rows)
    for q, (a, b) in enumerate(PAIRS):
        term = scaled[a] * other[b] + scaled[b] * other[a]
        rows[q : q + 1, :] = jnp.sum(term[:8] + term[8:16] + term[16:], axis=0, keepdims=True)
    total = jnp.sum(rows[...], axis=1, keepdims=True) + jnp.sum(sums[...], axis=1, keepdims=True)
    picked = lax.broadcasted_iota(jnp.int32, (16, 128), 0) + 64 == lanes(16, 128)
    note = jnp.sum(jnp.where(picked, total, 0.0), axis=0, keepdims=True)
    for h in range(2):
        turned = []
        for c in range(NB * THIRDS):
            t, b = c // NB, c % NB
            value = returned[b * 24 + t * 8 : b * 24 + t * 8 + 8, h * 128 : h * 128 + 128]
            turned.append(turn(value, COLS * (c if c < 10 else c - 10)))
        for k in range(8):
            p = 8 * h + k
            value = turned[0]
            for c in range(1, 10):
                value = jnp.where(masks[k + c], turned[c], value)
            out[p * 8 : p * 8 + 8, :] = turn(value, -COLS * k)
            more[p * 8 : p * 8 + 8, :] = turn(jnp.where(masks[k + 1], turned[11], turned[10]), -COLS * k)
    pieces = [more[pl.ds(i, PENCIL, stride=8), :] for i in range(FIRSTS)]
    out[pl.ds(6, PENCIL, stride=8), :] = gathered(pieces[:5], 24, 0)
    out[pl.ds(7, PENCIL, stride=8), :] = jnp.where(lanes(PENCIL, 128) < 24, pieces[5], note)


def back_first(given, table, out):
    result = dot(table[...], jnp.concatenate([given[pl.ds(i, PENCIL, stride=8), :] for i in range(FIRSTS)], axis=0))
    for i in range(ROWS):
        out[pl.ds(i, SLAB, stride=8), :] = result[i * SLAB : (i + 1) * SLAB]
    rest = [given[pl.ds(i, PENCIL, stride=8), :] for i in (6, 7)]
    result = dot(table[...], jnp.concatenate([turn(rest[i // 5], -24 * (i % 5)) for i in range(FIRSTS)], axis=0))
    pieces = [result[i * SLAB : (i + 1) * SLAB] for i in range(ROWS)]
    out[pl.ds(6, SLAB, stride=8), :] = gathered(pieces[:5], 24, 0)
    note = jnp.sum(rest[1], axis=0, keepdims=True)
    out[pl.ds(7, SLAB, stride=8), :] = jnp.where(lanes(SLAB, 128) < 24, pieces[5], note)


def back_third(given, local, table, out, lines, low, high, sent):
    rest = [given[pl.ds(i, SLAB, stride=8), :] for i in (6, 7)]
    for i in range(ROWS):
        value = given[pl.ds(i, SLAB, stride=8), :]
        at = i * HALF
        lines[0:32, at : at + HALF] = value[:, :HALF]
        lines[32:64, at : at + HALF] = value[:, HALF:WIDE]
        lines[64:96, at : at + 24] = value[:, WIDE : WIDE + 24]
        lines[64:96, at + 24 : at + HALF] = rest[i // 5][:, 24 * (i % 5) : 24 * (i % 5) + 24]
    kinetic_part = dot(lines[...], table[...], ((0,), (0,)))
    note = jnp.sum(rest[1], axis=0, keepdims=True) * (1.0 / CELLS)
    factor, inverse = {}, {}
    for q, (a, b) in enumerate(PAIRS):
        value = note[:, 64 + q : 65 + q]
        for c in range(b):
            value = value - factor[a, c] * factor[b, c]
        if a == b:
            factor[a, a] = jnp.sqrt(value)
            inverse[a] = 1.0 / factor[a, a]
        else:
            factor[a, b] = value * inverse[b]
    copies = [pltpu.make_async_copy(low.at[i], out.at[i, :, :, 0:128], sent.at[i]) for i in range(ROWS)]
    copies += [pltpu.make_async_copy(high.at[i], out.at[i, :, :, 128:NG], sent.at[ROWS + i]) for i in range(ROWS)]
    low, high = low.reshape(ROWS * COLS * NB, 128), high.reshape(ROWS * COLS * NB, 64)
    for i in range(ROWS):
        done = []
        for a in range(NB):
            value = local[a, i] + kinetic_part[i * HALF + a * COLS : i * HALF + a * COLS + COLS]
            for b in range(a):
                value = value - factor[a, b] * done[b]
            value = value * inverse[a]
            done.append(value)
            rows = pl.ds(i * HALF + a, COLS, stride=NB)
            low[rows, :] = value[:, :128]
            high[rows, :] = value[:, 128:]
        copies[i].start()
        copies[ROWS + i].start()
    for copy in copies:
        copy.wait()


def f32(*shape):
    return jax.ShapeDtypeStruct(shape, jnp.float32)


def held(*shape):
    return pltpu.VMEM(shape, jnp.float32)


def call(body, kinds, outs, scratch=()):
    places = {"k": pltpu.VMEM, "h": pl.ANY}
    whole = [jax.tree.map(lambda _: pl.BlockSpec(memory_space=pltpu.VMEM), outs), pl.BlockSpec(memory_space=pl.ANY)]
    made = pl.pallas_call(
        body,
        out_shape=outs,
        in_specs=[pl.BlockSpec(memory_space=places[kind]) for kind in kinds],
        out_specs=whole[isinstance(outs, jax.ShapeDtypeStruct)],
        scratch_shapes=[pltpu.VMEM(shape, jnp.float32) if isinstance(shape, tuple) else shape for shape in scratch],
        name=body.__name__,
    )

    def run(*given):
        return made(*[pltpu.with_memory_space_constraint(x, places[kind]) for kind, x in zip(kinds, given)])

    return run


def trade(value, axis, number):
    blocks = value.reshape(number, -1, 8 if value.shape[0] % (8 * number) == 0 else 2, 128)
    return lax.all_to_all(blocks, axis, split_axis=0, concat_axis=0, tiled=True).reshape(value.shape)


def local_step(orbitals, potential, unlocked):
    third, first, first_back, second, second_back = tables()
    outs = (held(SLAB * 14, 128), held(NB, ROWS, COLS, NG), held(16, NG))
    scratch = [pltpu.SMEM((NB,), jnp.int32)] + [(ROWS, COLS, NB, 128), (ROWS, COLS, NB, 64), (ROWS, COLS, NG), (MODES, NG), (ROWS * WIDE, NG)]
    made = call(forward_third, "hhhh", outs, scratch + [pltpu.SemaphoreType.DMA((2 * ROWS + 3,))])
    spectrum, local, sums = made(unlocked, orbitals.transpose(1, 2, 0, 3), potential, third)
    spectrum = trade(spectrum, "slab", SLAB)
    spectrum = trade(call(forward_first, "kk", held(PENCIL * 14, 128))(spectrum, first), "pencil", PENCIL)
    scratch = [(THIRDS * 128, 128), (8 * 24, 256), (PENCIL * 8, 128), (16, 128)]
    made = call(middle, "kkkk", held(PENCIL * 8, 128), scratch)
    spectrum = trade(made(spectrum, sums, second, second_back), "pencil", PENCIL)
    spectrum = trade(call(back_first, "kk", held(SLAB * 8, 128))(spectrum, first_back), "slab", SLAB)
    scratch = [(MODES, ROWS * HALF), (ROWS, COLS, NB, 128), (ROWS, COLS, NB, 64), pltpu.SemaphoreType.DMA((2 * ROWS,))]
    made = call(back_third, "kkk", f32(ROWS, COLS, NB, NG), scratch)
    return made(spectrum, local, third).transpose(2, 0, 1, 3)


def solution(mesh):
    in_specs = (P(None, "slab", "pencil", None), P("slab", "pencil", None), P())
    out_specs = P(None, "slab", "pencil", None)
    return jax.shard_map(local_step, mesh=mesh, in_specs=in_specs, out_specs=out_specs, check_vma=False)
```

```python
import functools

import jax
import jax.numpy as jnp
import numpy as np
from jax import lax
from jax.experimental import pallas as pl
from jax.experimental.pallas import tpu as pltpu
from jax.sharding import PartitionSpec as P

NG = 192
NB = 4
CUT = NG // 4
MODES = 2 * CUT
SLAB = 32
PENCIL = 16
ROWS = NG // SLAB
COLS = NG // PENCIL
CELLS = float(NG**3)
THIRDS = MODES // SLAB
FIRSTS = MODES // PENCIL
WIDE = 2 * NB * COLS
HALF = NB * COLS
PAIRS = [(a, b) for a in range(NB) for b in range(a + 1)]
highest = lax.Precision.HIGHEST

SLOTS = 16
SPLIT = 9
SPECIAL = 2


def basis():
    place = np.arange(NG)
    mode = np.arange(MODES)
    angle = 2.0 * np.pi / NG * ((mode[:, None] % CUT) * place[None, :] % NG)
    return np.where(mode[:, None] < CUT, np.cos(angle), np.sin(angle))


def thirds(rank):
    return [(start + way * (rank // 2)) + CUT * (rank % 2) for start, way in ((15, -1), (16, 1), (32, 1))]


def below(limit):
    return [m for m in range(MODES) if m % CUT < limit and m != CUT]


def slots():
    kinds = [[0] * PENCIL] * 6 + [[1] * PENCIL] * 5 + [[1] * SPLIT + [2] * (PENCIL - SPLIT)] + [[2] * PENCIL] * 4
    queues = [below(47) + [CUT, 47, 95], below(45), below(36)]
    firsts = [[queues[kinds[slot][p]].pop(0) for p in range(PENCIL)] for slot in range(SLOTS)]
    assert not any(queues)
    return np.array(kinds), np.array(firsts), {PENCIL - 2: 45, PENCIL - 1: 93}


def mode_table():
    kinds, firsts, others = slots()
    table = np.zeros((SLAB, PENCIL, 128))
    weight = np.where(np.arange(MODES) == 0, 1.0, np.where(np.arange(MODES) == CUT, 0.0, 2.0))
    for rank in range(SLAB):
        for p in range(PENCIL):
            for slot in range(SLOTS):
                kind, first = kinds[slot, p], firsts[slot, p]
                if rank < SPECIAL and slot == 5 and p in others:
                    kind, first = 1, others[p]
                third = thirds(rank)[kind]
                table[rank, p, slot] = (third % CUT) ** 2 + (first % CUT) ** 2
                table[rank, p, SLOTS + slot] = weight[third] * weight[first] / CELLS
    return table.reshape(SLAB * PENCIL, 128)


def tables():
    real = basis()
    third = np.concatenate([real[[thirds(rank)[t] for rank in range(SLAB)]] for t in range(THIRDS)])
    kinds, firsts, others = slots()
    lines = real.reshape(MODES, SLAB, ROWS).transpose(0, 2, 1).reshape(MODES, NG)
    rows = [np.where((kinds == t)[:, :, None], lines[firsts], 0.0) for t in range(THIRDS)]
    extra = np.zeros((PENCIL, NG))
    for p, m in others.items():
        extra[p] = lines[m]
    parts = [rows[0][0:6], np.concatenate([rows[1][6:12], extra[None]]), rows[2][11:16]]
    parts = [part.reshape(-1, NG) for part in parts]
    second = np.zeros((128, 2, 128))
    second[:MODES, :, : NG // 2] = real.reshape(MODES, 2, NG // 2)
    second = second.reshape(128, 256)
    made = [third, np.concatenate(parts), *[part.T for part in parts], second.T, second, mode_table()]
    return [np.ascontiguousarray(t, dtype=np.float32) for t in made]


def dot(a, b, dims=((1,), (0,))):
    return lax.dot_general(a, b, (dims, ((), ())), precision=highest, preferred_element_type=jnp.float32)


def lanes(*shape):
    return lax.broadcasted_iota(jnp.int32, shape, len(shape) - 1)


def turn(value, by):
    by = by % 128
    return pltpu.roll(value, by, 1) if by else value


def gathered(pieces, width, start):
    lane = lanes(*pieces[0].shape)
    result = jnp.zeros(pieces[0].shape, jnp.float32)
    for k, piece in enumerate(pieces):
        here = (lane >= k * width) & (lane < k * width + width)
        result = jnp.where(here, turn(piece, k * width - start), result)
    return result


def forward_third(flags, orbitals, potential, table, out, local, sums, kind, low, high, field, made, lines, ready):
    copies = [pltpu.make_async_copy(flags, kind, ready.at[0]), pltpu.make_async_copy(potential, field, ready.at[1])]
    copies += [pltpu.make_async_copy(orbitals.at[i, :, :, 0:128], low.at[i], ready.at[2 + i]) for i in range(ROWS)]
    copies += [pltpu.make_async_copy(orbitals.at[i, :, :, 128:NG], high.at[i], ready.at[2 + ROWS + i]) for i in range(ROWS)]
    copies.append(pltpu.make_async_copy(table, made, ready.at[2 + 2 * ROWS]))
    low, high = low.reshape(ROWS * COLS * NB, 128), high.reshape(ROWS * COLS * NB, 64)
    for copy in copies:
        copy.start()
    copies[0].wait()
    copies[1].wait()
    totals = [None] * len(PAIRS)
    for i in range(ROWS):
        copies[2 + i].wait()
        copies[2 + ROWS + i].wait()
        shifted = (field[i] - 1.0) * (1.0 / 1.5)
        own = []
        for b in range(NB):
            base = i * WIDE + b * COLS
            parts = [ref[pl.ds(i * WIDE // 2 + b, COLS, stride=NB), :] for ref in (low, high)]
            value = jnp.concatenate([parts[0], parts[1]], axis=1)
            kept = jnp.where(kind[b] == 1, value * shifted, value)
            lines[base : base + COLS, :] = value * jnp.where(kind[b] == 1, 1.0 / 1.5, 0.0)
            lines[base + HALF : base + HALF + COLS, :] = kept
            local[b, i] = kept
            own.append(kept)
        for q, (a, b) in enumerate(PAIRS):
            term = own[a] * own[b]
            totals[q] = term if totals[q] is None else totals[q] + term
    copies[-1].wait()
    whole = lanes(SLAB, 128)
    last = []
    for i in range(ROWS):
        if i % 2 == 0:
            spectrum = dot(made[...], lines[i * WIDE : i * WIDE + 2 * WIDE, :], ((1,), (1,)))
            result = spectrum[:, :128]
        else:
            more = jnp.concatenate([spectrum[:, 128:], jnp.zeros((MODES, 64), jnp.float32)], axis=1)
            result = jnp.where(lanes(MODES, 128) < 32, turn(spectrum[:, :128], 32), turn(more, 32))
        parts = [result[t * 32 : t * 32 + 32] for t in range(THIRDS)]
        for t in range(2):
            extra = turn(parts[2], WIDE - 32 * t)
            out[pl.ds(t * 7 + i, SLAB, stride=14), :] = jnp.where(whole < WIDE, parts[t], extra)
        last.append(parts[2])
    sums[...] = jnp.zeros_like(sums)
    for q in range(len(PAIRS)):
        sums[q : q + 1, :] = jnp.sum(totals[q], axis=0, keepdims=True)
    for t in range(2):
        out[pl.ds(t * 7 + 6, SLAB, stride=14), :] = gathered(last[t * 4 : t * 4 + 4], 32, 64)


def shared(number):
    row = lax.broadcasted_iota(jnp.int32, (PENCIL, number), 0)
    return (row >= PENCIL - 2) & (lax.axis_index("slab") < SPECIAL)


def forward_first(given, table, out):
    blocks = [[given[pl.ds(t * 7 + i, SLAB, stride=14), :] for i in range(ROWS)] for t in range(2)]
    rest = [given[pl.ds(t * 7 + 6, SLAB, stride=14), :] for t in range(2)]
    lane = lanes(SLAB, 128)
    last = []
    for i in range(ROWS):
        value = jnp.where(lane < 64, turn(blocks[1][i], 64), turn(rest[i // 4], 64 - 32 * (i % 4)))
        last.append(jnp.where(lane < 32, turn(blocks[0][i], 32), value))
    low = dot(table[0:96, :], jnp.concatenate(blocks[0], axis=0))
    middle = dot(table[96:208, :], jnp.concatenate(blocks[1], axis=0))
    high = dot(table[208:288, :], jnp.concatenate(last, axis=0))
    parts = [low[i * 16 : i * 16 + 16] for i in range(6)] + [middle[i * 16 : i * 16 + 16] for i in range(6)]
    parts[5] = jnp.where(shared(128), middle[96:112], parts[5])
    parts[11] = parts[11] + high[0:16]
    parts += [high[i * 16 : i * 16 + 16] for i in range(1, 5)]
    lane = lanes(PENCIL, 128)
    for i in range(12):
        more = turn(parts[12 + i // 3], WIDE - 32 * (i % 3))
        out[pl.ds(i, PENCIL, stride=12), :] = jnp.where(lane < WIDE, parts[i], more)


def middle(given, sums, modes, forward, back, out, tiles, lines, rows):
    parts = [given[pl.ds(i, PENCIL, stride=12), :] for i in range(12)]
    parts += [gathered(parts[3 * i : 3 * i + 3], 32, WIDE) for i in range(4)]
    for slot in range(SLOTS):
        tiles[pl.ds(slot // 8 * 128 + slot % 8, PENCIL, stride=8), :] = parts[slot]
    lane = lanes(8, 128)
    masks = [((lane - COLS * m) & 127) < COLS for m in range(15)]
    for h in range(2):
        for t in range(2):
            turned = []
            for k in range(8):
                at = t * 128 + (8 * h + k) * 8
                turned.append(turn(tiles[at : at + 8, :], COLS * k))
            for u in range(2 * NB):
                value = turned[0]
                for k in range(1, 8):
                    value = jnp.where(masks[k + u], turned[k], value)
                at = u * SLOTS + t * 8
                lines[at : at + 8, h * 128 : h * 128 + 128] = turn(value, -COLS * u)
    spectrum = dot(lines[...], forward[...])
    lane = lanes(SLOTS, 128)
    own = modes[pl.ds(lax.axis_index("slab") * PENCIL + lax.axis_index("pencil"), 1), :]
    row = lax.broadcasted_iota(jnp.int32, (SLOTS, 128), 0)
    squared = jnp.sum(jnp.where(lane == row, own, 0.0), axis=1, keepdims=True)
    weight = jnp.sum(jnp.where(lane == row + SLOTS, own, 0.0), axis=1, keepdims=True)
    size = jnp.where(lane < CUT, lane, lane - CUT)
    squared = squared + (size * size).astype(jnp.float32)
    kinetic = jnp.where((lane < MODES) & (squared < float(CUT * CUT)), squared * (4.0 / CUT**2), 0.0)
    weight = weight * jnp.where(lane == 0, 1.0, jnp.where(lane == CUT, 0.0, 2.0)) * kinetic
    scaled, other = [], []
    for b in range(NB):
        value = spectrum[b * SLOTS : (b + 1) * SLOTS]
        scaled.append(value * weight)
        other.append(0.5 * kinetic * value + spectrum[(NB + b) * SLOTS : (NB + b + 1) * SLOTS])
    returned = dot(jnp.concatenate(scaled, axis=0), back[...])
    rows[...] = jnp.zeros_like(rows)
    for q, (a, b) in enumerate(PAIRS):
        term = scaled[a] * other[b] + scaled[b] * other[a]
        rows[q : q + 1, :] = jnp.sum(term, axis=0, keepdims=True)
    total = jnp.sum(rows[...], axis=1, keepdims=True) + jnp.sum(sums[...], axis=1, keepdims=True)
    note = jnp.sum(jnp.where(lane == row + WIDE, total, 0.0), axis=0, keepdims=True)
    lane = lanes(8, 128)
    for h in range(2):
        turned = []
        for c in range(2 * NB):
            at = c % NB * SLOTS + c // NB * 8
            turned.append(turn(returned[at : at + 8, h * 128 : h * 128 + 128], COLS * c))
        for k in range(8):
            p = 8 * h + k
            value = turned[0]
            for c in range(1, 2 * NB):
                value = jnp.where(masks[k + c], turned[c], value)
            out[p * 8 : p * 8 + 8, :] = jnp.where(lane < WIDE, turn(value, -COLS * k), note)


def back_first(given, low, middle, high, out):
    parts = [given[pl.ds(i, PENCIL, stride=8), :] for i in range(8)]
    note = jnp.sum(parts[0], axis=0, keepdims=True)
    parts += [turn(part, -HALF) for part in parts]
    empty = jnp.zeros((PENCIL, 128), jnp.float32)
    here = shared(128)
    own = [*parts[0:5], jnp.where(here, empty, parts[5])]
    first = dot(low[...], jnp.concatenate(own, axis=0))
    second = dot(middle[...], jnp.concatenate([*parts[6:12], jnp.where(here, parts[5], empty)], axis=0))
    third = dot(high[...], jnp.concatenate(parts[11:16], axis=0))
    lane = lanes(SLAB, 128)
    pieces = []
    for i in range(ROWS):
        rows = slice(i * SLAB, (i + 1) * SLAB)
        value = jnp.where(lane < WIDE, turn(second[rows], HALF), turn(third[rows], WIDE))
        out[pl.ds(i, SLAB, stride=8), :] = jnp.where(lane < HALF, first[rows], value)
        pieces.append(third[rows])
    out[pl.ds(6, SLAB, stride=8), :] = gathered(pieces[:5], 24, 24)
    out[pl.ds(7, SLAB, stride=8), :] = jnp.where(lane < 24, turn(pieces[5], -24), note)


def back_third(given, local, table, out, lines, low, high, sent):
    rest = [given[pl.ds(i, SLAB, stride=8), :] for i in (6, 7)]
    for i in range(ROWS):
        value = given[pl.ds(i, SLAB, stride=8), :]
        at = i * HALF
        lines[0:32, at : at + HALF] = value[:, :HALF]
        lines[32:64, at : at + HALF] = value[:, HALF:WIDE]
        lines[64:96, at : at + 24] = value[:, WIDE : WIDE + 24]
        lines[64:96, at + 24 : at + HALF] = rest[i // 5][:, 24 * (i % 5) : 24 * (i % 5) + 24]
    kinetic_part = dot(lines[...], table[...], ((0,), (0,)))
    note = jnp.sum(rest[1], axis=0, keepdims=True) * (1.0 / CELLS)
    factor, inverse = {}, {}
    for q, (a, b) in enumerate(PAIRS):
        value = note[:, WIDE + q : WIDE + q + 1]
        for c in range(b):
            value = value - factor[a, c] * factor[b, c]
        if a == b:
            factor[a, a] = jnp.sqrt(value)
            inverse[a] = 1.0 / factor[a, a]
        else:
            factor[a, b] = value * inverse[b]
    copies = [pltpu.make_async_copy(low.at[i], out.at[i, :, :, 0:128], sent.at[i]) for i in range(ROWS)]
    copies += [pltpu.make_async_copy(high.at[i], out.at[i, :, :, 128:NG], sent.at[ROWS + i]) for i in range(ROWS)]
    low, high = low.reshape(ROWS * COLS * NB, 128), high.reshape(ROWS * COLS * NB, 64)
    for i in range(ROWS):
        done = []
        for a in range(NB):
            value = local[a, i] + kinetic_part[i * HALF + a * COLS : i * HALF + a * COLS + COLS]
            for b in range(a):
                value = value - factor[a, b] * done[b]
            value = value * inverse[a]
            done.append(value)
            rows = pl.ds(i * HALF + a, COLS, stride=NB)
            low[rows, :] = value[:, :128]
            high[rows, :] = value[:, 128:]
        copies[i].start()
        copies[ROWS + i].start()
    for copy in copies:
        copy.wait()


def f32(*shape):
    return jax.ShapeDtypeStruct(shape, jnp.float32)


def held(*shape):
    return pltpu.VMEM(shape, jnp.float32)


def call(body, kinds, outs, scratch=()):
    places = {"k": pltpu.VMEM, "h": pl.ANY}
    whole = [jax.tree.map(lambda _: pl.BlockSpec(memory_space=pltpu.VMEM), outs), pl.BlockSpec(memory_space=pl.ANY)]
    made = pl.pallas_call(
        body,
        out_shape=outs,
        in_specs=[pl.BlockSpec(memory_space=places[kind]) for kind in kinds],
        out_specs=whole[isinstance(outs, jax.ShapeDtypeStruct)],
        scratch_shapes=[pltpu.VMEM(shape, jnp.float32) if isinstance(shape, tuple) else shape for shape in scratch],
        name=body.__name__,
    )

    def run(*given):
        return made(*[pltpu.with_memory_space_constraint(x, places[kind]) for kind, x in zip(kinds, given)])

    return run


def trade(value, axis, number):
    rows = next(size for size in (8, 4, 2) if value.shape[0] % (size * number) == 0)
    blocks = value.reshape(number, -1, rows, 128)
    return lax.all_to_all(blocks, axis, split_axis=0, concat_axis=0, tiled=True).reshape(value.shape)


def local_step(orbitals, potential, unlocked):
    third, first, low, middle_back, high, second, second_back, modes = tables()
    outs = (held(SLAB * 14, 128), held(NB, ROWS, COLS, NG), held(16, NG))
    scratch = [pltpu.SMEM((NB,), jnp.int32)] + [(ROWS, COLS, NB, 128), (ROWS, COLS, NB, 64), (ROWS, COLS, NG), (MODES, NG), (ROWS * WIDE, NG)]
    made = call(forward_third, "hhhh", outs, scratch + [pltpu.SemaphoreType.DMA((2 * ROWS + 3,))])
    spectrum, local, sums = made(unlocked, orbitals.transpose(1, 2, 0, 3), potential, third)
    spectrum = trade(spectrum, "slab", SLAB)
    spectrum = trade(call(forward_first, "kk", held(PENCIL * 12, 128))(spectrum, first), "pencil", PENCIL)
    made = call(middle, "kkkkk", held(PENCIL * 8, 128), [(256, 128), (2 * NB * SLOTS, 256), (16, 128)])
    spectrum = trade(made(spectrum, sums, modes, second, second_back), "pencil", PENCIL)
    made = call(back_first, "kkkk", held(SLAB * 8, 128))
    spectrum = trade(made(spectrum, low, middle_back, high), "slab", SLAB)
    scratch = [(MODES, ROWS * HALF), (ROWS, COLS, NB, 128), (ROWS, COLS, NB, 64), pltpu.SemaphoreType.DMA((2 * ROWS,))]
    made = call(back_third, "kkk", f32(ROWS, COLS, NB, NG), scratch)
    return made(spectrum, local, third).transpose(2, 0, 1, 3)


def solution(mesh):
    in_specs = (P(None, "slab", "pencil", None), P("slab", "pencil", None), P())
    out_specs = P(None, "slab", "pencil", None)
    return jax.shard_map(local_step, mesh=mesh, in_specs=in_specs, out_specs=out_specs, check_vma=False)
```

```python
import functools

import jax
import jax.numpy as jnp
import numpy as np
from jax import lax
from jax.experimental import pallas as pl
from jax.experimental.pallas import tpu as pltpu
from jax.sharding import PartitionSpec as P

NG = 192
NB = 4
CUT = NG // 4
MODES = 2 * CUT
SLAB = 32
PENCIL = 16
ROWS = NG // SLAB
COLS = NG // PENCIL
CELLS = float(NG**3)
THIRDS = MODES // SLAB
FIRSTS = MODES // PENCIL
WIDE = 2 * NB * COLS
HALF = NB * COLS
PAIRS = [(a, b) for a in range(NB) for b in range(a + 1)]
highest = lax.Precision.HIGHEST

SLOTS = 16
SPLIT = 9
SPECIAL = 2


def basis():
    place = np.arange(NG)
    mode = np.arange(MODES)
    angle = 2.0 * np.pi / NG * ((mode[:, None] % CUT) * place[None, :] % NG)
    return np.where(mode[:, None] < CUT, np.cos(angle), np.sin(angle))


def thirds(rank):
    return [(start + way * (rank // 2)) + CUT * (rank % 2) for start, way in ((15, -1), (16, 1), (32, 1))]


def below(limit):
    return [m for m in range(MODES) if m % CUT < limit and m != CUT]


def slots():
    kinds = [[0] * PENCIL] * 6 + [[1] * PENCIL] * 5 + [[1] * SPLIT + [2] * (PENCIL - SPLIT)] + [[2] * PENCIL] * 4
    queues = [below(47) + [CUT, 47, 95], below(45), below(36)]
    firsts = [[queues[kinds[slot][p]].pop(0) for p in range(PENCIL)] for slot in range(SLOTS)]
    assert not any(queues)
    return np.array(kinds), np.array(firsts), {PENCIL - 2: 45, PENCIL - 1: 93}


def mode_table():
    kinds, firsts, others = slots()
    table = np.zeros((SLAB, PENCIL, 128))
    weight = np.where(np.arange(MODES) == 0, 1.0, np.where(np.arange(MODES) == CUT, 0.0, 2.0))
    for rank in range(SLAB):
        for p in range(PENCIL):
            for slot in range(SLOTS):
                kind, first = kinds[slot, p], firsts[slot, p]
                if rank < SPECIAL and slot == 5 and p in others:
                    kind, first = 1, others[p]
                third = thirds(rank)[kind]
                table[rank, p, slot] = (third % CUT) ** 2 + (first % CUT) ** 2
                table[rank, p, SLOTS + slot] = weight[third] * weight[first] / CELLS
    return table.reshape(SLAB * PENCIL, 128)


def tables():
    real = basis()
    third = np.concatenate([real[[thirds(rank)[t] for rank in range(SLAB)]] for t in range(THIRDS)])
    kinds, firsts, others = slots()
    lines = real.reshape(MODES, SLAB, ROWS).transpose(0, 2, 1).reshape(MODES, NG)
    rows = [np.where((kinds == t)[:, :, None], lines[firsts], 0.0) for t in range(THIRDS)]
    extra = np.zeros((PENCIL, NG))
    for p, m in others.items():
        extra[p] = lines[m]
    parts = [rows[0][0:6], np.concatenate([rows[1][6:12], extra[None]]), rows[2][11:16]]
    parts = [part.reshape(-1, NG) for part in parts]
    second = np.zeros((128, 2, 128))
    second[:MODES, :, : NG // 2] = real.reshape(MODES, 2, NG // 2)
    second = second.reshape(128, 256)
    every = lines[firsts]
    back = every.reshape(-1, NG).T.copy()
    for p, m in others.items():
        every[5, p] = lines[m]
    special = every.reshape(-1, NG).T[:, 0:128]
    made = [third, np.concatenate(parts), back, special, second.T, second, mode_table()]
    return [np.ascontiguousarray(t, dtype=np.float32) for t in made]


def dot(a, b, dims=((1,), (0,))):
    return lax.dot_general(a, b, (dims, ((), ())), precision=highest, preferred_element_type=jnp.float32)


def lanes(*shape):
    return lax.broadcasted_iota(jnp.int32, shape, len(shape) - 1)


def turn(value, by):
    by = by % 128
    return pltpu.roll(value, by, 1) if by else value


def gathered(pieces, width, start):
    lane = lanes(*pieces[0].shape)
    result = jnp.zeros(pieces[0].shape, jnp.float32)
    for k, piece in enumerate(pieces):
        here = (lane >= k * width) & (lane < k * width + width)
        result = jnp.where(here, turn(piece, k * width - start), result)
    return result


def forward_third(flags, orbitals, potential, table, out, local, sums, kind, low, high, field, made, lines, ready):
    copies = [pltpu.make_async_copy(flags, kind, ready.at[0]), pltpu.make_async_copy(potential, field, ready.at[1])]
    copies += [pltpu.make_async_copy(orbitals.at[i, :, :, 0:128], low.at[i], ready.at[2 + i]) for i in range(ROWS)]
    copies += [pltpu.make_async_copy(orbitals.at[i, :, :, 128:NG], high.at[i], ready.at[2 + ROWS + i]) for i in range(ROWS)]
    copies.append(pltpu.make_async_copy(table, made, ready.at[2 + 2 * ROWS]))
    low, high = low.reshape(ROWS * COLS * NB, 128), high.reshape(ROWS * COLS * NB, 64)
    for copy in copies:
        copy.start()
    copies[0].wait()
    copies[1].wait()
    totals = [None] * len(PAIRS)
    for i in range(ROWS):
        copies[2 + i].wait()
        copies[2 + ROWS + i].wait()
        shifted = (field[i] - 1.0) * (1.0 / 1.5)
        own = []
        for b in range(NB):
            base = i * WIDE + b * COLS
            parts = [ref[pl.ds(i * WIDE // 2 + b, COLS, stride=NB), :] for ref in (low, high)]
            value = jnp.concatenate([parts[0], parts[1]], axis=1)
            kept = jnp.where(kind[b] == 1, value * shifted, value)
            lines[base : base + COLS, :] = value
            lines[base + HALF : base + HALF + COLS, :] = kept
            local[b, i] = kept
            own.append(kept)
        for q, (a, b) in enumerate(PAIRS):
            term = own[a] * own[b]
            totals[q] = term if totals[q] is None else totals[q] + term
    copies[-1].wait()
    whole = lanes(SLAB, 128)
    last = []
    lane = lanes(MODES, 128)
    scale = jnp.ones((MODES, 128), jnp.float32)
    for b in range(NB):
        alpha = jnp.where(kind[b] == 1, 1.0 / 1.5, 0.0)
        scale = jnp.where((lane >= b * COLS) & (lane < (b + 1) * COLS), alpha, scale)
    for i in range(ROWS):
        if i % 2 == 0:
            spectrum = dot(made[...], lines[i * WIDE : i * WIDE + 2 * WIDE, :], ((1,), (1,)))
            result = spectrum[:, :128]
        else:
            more = jnp.concatenate([spectrum[:, 128:], jnp.zeros((MODES, 64), jnp.float32)], axis=1)
            result = jnp.where(lanes(MODES, 128) < 32, turn(spectrum[:, :128], 32), turn(more, 32))
        result = result * scale
        parts = [result[t * 32 : t * 32 + 32] for t in range(THIRDS)]
        for t in range(2):
            extra = turn(parts[2], WIDE - 32 * t)
            out[pl.ds(t * 7 + i, SLAB, stride=14), :] = jnp.where(whole < WIDE, parts[t], extra)
        last.append(parts[2])
    sums[...] = jnp.zeros_like(sums)
    for q in range(len(PAIRS)):
        sums[q : q + 1, :] = jnp.sum(totals[q], axis=0, keepdims=True)
    for t in range(2):
        out[pl.ds(t * 7 + 6, SLAB, stride=14), :] = gathered(last[t * 4 : t * 4 + 4], 32, 64)


def shared(number):
    row = lax.broadcasted_iota(jnp.int32, (PENCIL, number), 0)
    return (row >= PENCIL - 2) & (lax.axis_index("slab") < SPECIAL)


def forward_first(given, table, out):
    blocks = [[given[pl.ds(t * 7 + i, SLAB, stride=14), :] for i in range(ROWS)] for t in range(2)]
    rest = [given[pl.ds(t * 7 + 6, SLAB, stride=14), :] for t in range(2)]
    lane = lanes(SLAB, 128)
    last = []
    for i in range(ROWS):
        value = jnp.where(lane < 64, turn(blocks[1][i], 64), turn(rest[i // 4], 64 - 32 * (i % 4)))
        last.append(jnp.where(lane < 32, turn(blocks[0][i], 32), value))
    low = dot(table[0:96, :], jnp.concatenate(blocks[0], axis=0))
    middle = dot(table[96:208, :], jnp.concatenate(blocks[1], axis=0))
    high = dot(table[208:288, :], jnp.concatenate(last, axis=0))
    parts = [low[i * 16 : i * 16 + 16] for i in range(6)] + [middle[i * 16 : i * 16 + 16] for i in range(6)]
    parts[5] = jnp.where(shared(128), middle[96:112], parts[5])
    parts[11] = parts[11] + high[0:16]
    parts += [high[i * 16 : i * 16 + 16] for i in range(1, 5)]
    lane = lanes(PENCIL, 128)
    for i in range(12):
        more = turn(parts[12 + i // 3], WIDE - 32 * (i % 3))
        out[pl.ds(i, PENCIL, stride=12), :] = jnp.where(lane < WIDE, parts[i], more)


def middle(given, sums, modes, forward, back, out, tiles, lines, rows):
    parts = [given[pl.ds(i, PENCIL, stride=12), :] for i in range(12)]
    parts += [gathered(parts[3 * i : 3 * i + 3], 32, WIDE) for i in range(4)]
    for slot in range(SLOTS):
        tiles[pl.ds(slot // 8 * 128 + slot % 8, PENCIL, stride=8), :] = parts[slot]
    lane = lanes(8, 128)
    masks = [((lane - COLS * m) & 127) < COLS for m in range(15)]
    for h in range(2):
        for t in range(2):
            turned = []
            for k in range(8):
                at = t * 128 + (8 * h + k) * 8
                turned.append(turn(tiles[at : at + 8, :], COLS * k))
            for u in range(2 * NB):
                value = turned[0]
                for k in range(1, 8):
                    value = jnp.where(masks[k + u], turned[k], value)
                at = u * SLOTS + t * 8
                lines[at : at + 8, h * 128 : h * 128 + 128] = turn(value, -COLS * u)
    spectrum = dot(lines[...], forward[...])
    lane = lanes(SLOTS, 128)
    own = modes[pl.ds(lax.axis_index("slab") * PENCIL + lax.axis_index("pencil"), 1), :]
    row = lax.broadcasted_iota(jnp.int32, (SLOTS, 128), 0)
    squared = jnp.sum(jnp.where(lane == row, own, 0.0), axis=1, keepdims=True)
    weight = jnp.sum(jnp.where(lane == row + SLOTS, own, 0.0), axis=1, keepdims=True)
    size = jnp.where(lane < CUT, lane, lane - CUT)
    squared = squared + (size * size).astype(jnp.float32)
    kinetic = jnp.where((lane < MODES) & (squared < float(CUT * CUT)), squared * (4.0 / CUT**2), 0.0)
    weight = weight * jnp.where(lane == 0, 1.0, jnp.where(lane == CUT, 0.0, 2.0)) * kinetic
    scaled, other = [], []
    for b in range(NB):
        value = spectrum[b * SLOTS : (b + 1) * SLOTS]
        scaled.append(value * weight)
        other.append(0.5 * kinetic * value + spectrum[(NB + b) * SLOTS : (NB + b + 1) * SLOTS])
    returned = dot(jnp.concatenate(scaled, axis=0), back[...])
    rows[...] = jnp.zeros_like(rows)
    for q, (a, b) in enumerate(PAIRS):
        term = scaled[a] * other[b] + scaled[b] * other[a]
        rows[q : q + 1, :] = jnp.sum(term, axis=0, keepdims=True)
    total = jnp.sum(rows[...], axis=1, keepdims=True) + jnp.sum(sums[...], axis=1, keepdims=True)
    note = jnp.sum(jnp.where(lane == row + WIDE, total, 0.0), axis=0, keepdims=True)
    for h in range(2):
        turned = []
        for c in range(2 * NB):
            at = c % NB * SLOTS + c // NB * 8
            turned.append(turn(returned[at : at + 8, h * 128 : h * 128 + 128], COLS * c))
        for k in range(8):
            p = 8 * h + k
            value = turned[0]
            for c in range(1, 2 * NB):
                value = jnp.where(masks[k + c], turned[c], value)
            tiles[p * 8 : p * 8 + 8, :] = turn(value, -COLS * k)
    parts = [tiles[pl.ds(i, PENCIL, stride=8), :] for i in range(8)]
    lane = lanes(PENCIL, 128)
    for i in range(6):
        more = turn(parts[6 + i // 3], WIDE - 32 * (i % 3))
        out[pl.ds(i, PENCIL, stride=7), :] = jnp.where(lane < WIDE, parts[i], more)
    out[pl.ds(6, PENCIL, stride=7), :] = jnp.broadcast_to(note, (PENCIL, 128))


def back_first(given, table, special, out):
    parts = [given[pl.ds(i, PENCIL, stride=7), :] for i in range(6)]
    note = jnp.sum(given[pl.ds(6, PENCIL, stride=7), :], axis=0, keepdims=True)
    parts += [gathered(parts[3 * i : 3 * i + 3], 32, WIDE) for i in range(2)]
    parts += parts
    lane = lanes(PENCIL, 128)
    row = lax.broadcasted_iota(jnp.int32, (PENCIL, 128), 0)
    inside = [lane < HALF, (lane >= HALF) & (lane < WIDE), lane >= WIDE, lane < 16]
    main, more = [], []
    empty = jnp.zeros((PENCIL, 128), jnp.float32)
    for slot in range(SLOTS):
        moved = turn(parts[slot], HALF)
        if slot < 6:
            value = jnp.where(inside[0], parts[slot], 0.0)
            if slot == 5:
                value = jnp.where(shared(128), jnp.where(inside[1], moved, 0.0), value)
        else:
            value = jnp.where(inside[1], moved if slot < 8 else parts[slot], 0.0)
        rest = empty
        if slot > 10:
            late = jnp.where(inside[2], moved, 0.0)
            rest = jnp.where(inside[3], moved, 0.0)
            if slot == 11:
                late, rest = jnp.where(row < SPLIT, value, late), jnp.where(row < SPLIT, 0.0, rest)
            value = late
        main.append(value)
        more.append(rest)
    given_all = jnp.concatenate([jnp.concatenate(main, axis=0), jnp.concatenate(more, axis=0)], axis=1)
    first = jnp.where(lax.axis_index("slab") < SPECIAL, special[...], table[:, 0:128])
    result = dot(jnp.concatenate([first, table[:, 128:256]], axis=1), given_all)
    pieces = []
    for i in range(ROWS):
        out[pl.ds(i, SLAB, stride=7), :] = result[i * SLAB : (i + 1) * SLAB, 0:128]
        pieces.append(result[i * SLAB : (i + 1) * SLAB, 128:256])
    out[pl.ds(6, SLAB, stride=7), :] = jnp.where(lanes(SLAB, 128) < WIDE, gathered(pieces, 16, 0), note)


def back_third(given, local, table, out, lines):
    rest = given[pl.ds(6, SLAB, stride=7), :]
    for i in range(ROWS):
        value = given[pl.ds(i, SLAB, stride=7), :]
        at = i * HALF
        lines[0:32, at : at + HALF] = value[:, :HALF]
        lines[32:64, at : at + HALF] = value[:, HALF:WIDE]
        lines[64:96, at : at + 32] = value[:, WIDE:128]
        lines[64:96, at + 32 : at + HALF] = rest[:, 16 * i : 16 * i + 16]
    kinetic_part = dot(lines[...], table[...], ((0,), (0,)))
    note = jnp.sum(rest, axis=0, keepdims=True) * (1.0 / CELLS)
    factor, inverse = {}, {}
    for q, (a, b) in enumerate(PAIRS):
        value = note[:, WIDE + q : WIDE + q + 1]
        for c in range(b):
            value = value - factor[a, c] * factor[b, c]
        if a == b:
            factor[a, a] = jnp.sqrt(value)
            inverse[a] = 1.0 / factor[a, a]
        else:
            factor[a, b] = value * inverse[b]
    for i in range(ROWS):
        done = []
        for a in range(NB):
            value = local[a, i] + kinetic_part[i * HALF + a * COLS : i * HALF + a * COLS + COLS]
            for b in range(a):
                value = value - factor[a, b] * done[b]
            value = value * inverse[a]
            done.append(value)
            out[i, :, a, :] = value


def f32(*shape):
    return jax.ShapeDtypeStruct(shape, jnp.float32)


def held(*shape):
    return pltpu.VMEM(shape, jnp.float32)


def call(body, kinds, outs, scratch=()):
    places = {"k": pltpu.VMEM, "h": pl.ANY}
    made = pl.pallas_call(
        body,
        out_shape=outs,
        in_specs=[pl.BlockSpec(memory_space=places[kind]) for kind in kinds],
        out_specs=jax.tree.map(lambda _: pl.BlockSpec(memory_space=pltpu.VMEM), outs),
        scratch_shapes=[pltpu.VMEM(shape, jnp.float32) if isinstance(shape, tuple) else shape for shape in scratch],
        name=body.__name__,
    )

    def run(*given):
        return made(*[pltpu.with_memory_space_constraint(x, places[kind]) for kind, x in zip(kinds, given)])

    return run


def trade(value, axis, number):
    rows = next(size for size in (8, 4, 2, 1) if value.shape[0] % (size * number) == 0)
    blocks = value.reshape(number, -1, rows, 128)
    return lax.all_to_all(blocks, axis, split_axis=0, concat_axis=0, tiled=True).reshape(value.shape)


def local_step(orbitals, potential, unlocked):
    third, first, first_back, special, second, second_back, modes = tables()
    outs = (held(SLAB * 14, 128), held(NB, ROWS, COLS, NG), held(16, NG))
    scratch = [pltpu.SMEM((NB,), jnp.int32)] + [(ROWS, COLS, NB, 128), (ROWS, COLS, NB, 64), (ROWS, COLS, NG), (MODES, NG), (ROWS * WIDE, NG)]
    made = call(forward_third, "hhhh", outs, scratch + [pltpu.SemaphoreType.DMA((2 * ROWS + 3,))])
    spectrum, local, sums = made(unlocked, orbitals.transpose(1, 2, 0, 3), potential, third)
    spectrum = trade(spectrum, "slab", SLAB)
    spectrum = trade(call(forward_first, "kk", held(PENCIL * 12, 128))(spectrum, first), "pencil", PENCIL)
    made = call(middle, "kkkkk", held(PENCIL * 7, 128), [(256, 128), (2 * NB * SLOTS, 256), (16, 128)])
    spectrum = trade(made(spectrum, sums, modes, second, second_back), "pencil", PENCIL)
    made = call(back_first, "kkk", held(SLAB * 7, 128))
    spectrum = trade(made(spectrum, first_back, special), "slab", SLAB)
    made = call(back_third, "kkk", f32(ROWS, COLS, NB, NG), [(MODES, ROWS * HALF)])
    return made(spectrum, local, third).transpose(2, 0, 1, 3)


def solution(mesh):
    in_specs = (P(None, "slab", "pencil", None), P("slab", "pencil", None), P())
    out_specs = P(None, "slab", "pencil", None)
    return jax.shard_map(local_step, mesh=mesh, in_specs=in_specs, out_specs=out_specs, check_vma=False)
```

```python
import functools

import jax
import jax.numpy as jnp
import numpy as np
from jax import lax
from jax.experimental import pallas as pl
from jax.experimental.pallas import tpu as pltpu
from jax.sharding import PartitionSpec as P

NG = 192
NB = 4
CUT = NG // 4
MODES = 2 * CUT
SLAB = 32
PENCIL = 16
ROWS = NG // SLAB
COLS = NG // PENCIL
CELLS = float(NG**3)
THIRDS = MODES // SLAB
FIRSTS = MODES // PENCIL
WIDE = 2 * NB * COLS
HALF = NB * COLS
PAIRS = [(a, b) for a in range(NB) for b in range(a + 1)]
highest = lax.Precision.HIGHEST

SLOTS = 16
SPLIT = 9
SPECIAL = 2


def basis():
    place = np.arange(NG)
    mode = np.arange(MODES)
    angle = 2.0 * np.pi / NG * ((mode[:, None] % CUT) * place[None, :] % NG)
    return np.where(mode[:, None] < CUT, np.cos(angle), np.sin(angle))


def thirds(rank):
    return [(start + way * (rank // 2)) + CUT * (rank % 2) for start, way in ((15, -1), (16, 1), (32, 1))]


def below(limit):
    return [m for m in range(MODES) if m % CUT < limit and m != CUT]


def slots():
    kinds = [[0] * PENCIL] * 6 + [[1] * PENCIL] * 5 + [[1] * SPLIT + [2] * (PENCIL - SPLIT)] + [[2] * PENCIL] * 4
    queues = [below(47) + [CUT, 47, 95], below(45), below(36)]
    firsts = [[queues[kinds[slot][p]].pop(0) for p in range(PENCIL)] for slot in range(SLOTS)]
    assert not any(queues)
    return np.array(kinds), np.array(firsts), {PENCIL - 2: 45, PENCIL - 1: 93}


def mode_table():
    kinds, firsts, others = slots()
    table = np.zeros((SLAB, PENCIL, 128))
    weight = np.where(np.arange(MODES) == 0, 1.0, np.where(np.arange(MODES) == CUT, 0.0, 2.0))
    for rank in range(SLAB):
        for p in range(PENCIL):
            for slot in range(SLOTS):
                kind, first = kinds[slot, p], firsts[slot, p]
                if rank < SPECIAL and slot == 5 and p in others:
                    kind, first = 1, others[p]
                third = thirds(rank)[kind]
                table[rank, p, slot] = (third % CUT) ** 2 + (first % CUT) ** 2
                table[rank, p, SLOTS + slot] = weight[third] * weight[first] / CELLS
    return np.concatenate([table.reshape(SLAB * PENCIL, 128), np.zeros((8, 128))])


def tables():
    real = basis()
    third = np.concatenate([real[[thirds(rank)[t] for rank in range(SLAB)]] for t in range(THIRDS)])
    kinds, firsts, others = slots()
    lines = real.reshape(MODES, SLAB, ROWS).transpose(0, 2, 1).reshape(MODES, NG)
    rows = [np.where((kinds == t)[:, :, None], lines[firsts], 0.0) for t in range(THIRDS)]
    extra = np.zeros((PENCIL, NG))
    for p, m in others.items():
        extra[p] = lines[m]
    parts = [rows[0][0:6], np.concatenate([rows[1][6:12], extra[None]]), rows[2][11:16]]
    parts = [part.reshape(-1, NG) for part in parts]
    second = np.zeros((128, 2, 128))
    second[:MODES, :, : NG // 2] = real.reshape(MODES, 2, NG // 2)
    second = second.reshape(128, 256)
    every = lines[firsts]
    back = every.reshape(-1, NG).T.copy()
    for p, m in others.items():
        every[5, p] = lines[m]
    special = every.reshape(-1, NG).T[:, 0:128]
    made = [third, np.concatenate(parts), back, special, second.T, second, mode_table()]
    return [np.ascontiguousarray(t, dtype=np.float32) for t in made]


def dot(a, b, dims=((1,), (0,))):
    return lax.dot_general(a, b, (dims, ((), ())), precision=highest, preferred_element_type=jnp.float32)


def lanes(*shape):
    return lax.broadcasted_iota(jnp.int32, shape, len(shape) - 1)


def turn(value, by):
    by = by % 128
    return pltpu.roll(value, by, 1) if by else value


def gathered(pieces, width, start):
    lane = lanes(*pieces[0].shape)
    result = jnp.zeros(pieces[0].shape, jnp.float32)
    for k, piece in enumerate(pieces):
        here = (lane >= k * width) & (lane < k * width + width)
        result = jnp.where(here, turn(piece, k * width - start), result)
    return result


def forward_third(flags, orbitals, potential, table, out, local, sums, kind, low, high, field, made, lines, ready):
    copies = [pltpu.make_async_copy(flags, kind, ready.at[0]), pltpu.make_async_copy(potential, field, ready.at[1])]
    for i in range(ROWS):
        copies.append(pltpu.make_async_copy(orbitals.at[i, :, :, 0:128], low.at[i], ready.at[2 + 2 * i]))
        copies.append(pltpu.make_async_copy(orbitals.at[i, :, :, 128:NG], high.at[i], ready.at[3 + 2 * i]))
    copies.append(pltpu.make_async_copy(table, made, ready.at[2 + 2 * ROWS]))
    low, high = low.reshape((ROWS + 1) * COLS * NB, 128), high.reshape((ROWS + 1) * COLS * NB, 64)
    for copy in copies:
        copy.start()
    copies[0].wait()
    copies[1].wait()
    totals = [None] * len(PAIRS)
    for i in range(ROWS):
        copies[2 + 2 * i].wait()
        copies[3 + 2 * i].wait()
        shifted = (field[i] - 1.0) * (1.0 / 1.5)
        own = []
        for b in range(NB):
            base = i * WIDE + b * COLS
            parts = [ref[pl.ds(i * WIDE // 2 + b, COLS, stride=NB), :] for ref in (low, high)]
            value = jnp.concatenate([parts[0], parts[1]], axis=1)
            kept = jnp.where(kind[b] == 1, value * shifted, value)
            lines[base : base + COLS, :] = value
            lines[base + HALF : base + HALF + COLS, :] = kept
            local[b, i] = kept
            own.append(kept)
        for q, (a, b) in enumerate(PAIRS):
            term = own[a] * own[b]
            totals[q] = term if totals[q] is None else totals[q] + term
    copies[-1].wait()
    whole = lanes(SLAB, 128)
    last = []
    lane = lanes(MODES, 128)
    scale = jnp.ones((MODES, 128), jnp.float32)
    for b in range(NB):
        alpha = jnp.where(kind[b] == 1, 1.0 / 1.5, 0.0)
        scale = jnp.where((lane >= b * COLS) & (lane < (b + 1) * COLS), alpha, scale)
    for i in range(ROWS):
        if i % 2 == 0:
            spectrum = dot(made[...], lines[i * WIDE : i * WIDE + 2 * WIDE, :], ((1,), (1,)))
            result = spectrum[:, :128]
        else:
            more = jnp.concatenate([spectrum[:, 128:], jnp.zeros((MODES, 64), jnp.float32)], axis=1)
            result = jnp.where(lanes(MODES, 128) < 32, turn(spectrum[:, :128], 32), turn(more, 32))
        result = result * scale
        parts = [result[t * 32 : t * 32 + 32] for t in range(THIRDS)]
        for t in range(2):
            extra = turn(parts[2], WIDE - 32 * t)
            out[pl.ds(t * 7 + i, SLAB, stride=14), :] = jnp.where(whole < WIDE, parts[t], extra)
        last.append(parts[2])
    sums[...] = jnp.zeros_like(sums)
    for q in range(len(PAIRS)):
        sums[q : q + 1, :] = jnp.sum(totals[q], axis=0, keepdims=True)
    for t in range(2):
        out[pl.ds(t * 7 + 6, SLAB, stride=14), :] = gathered(last[t * 4 : t * 4 + 4], 32, 64)


def shared(number):
    row = lax.broadcasted_iota(jnp.int32, (PENCIL, number), 0)
    return (row >= PENCIL - 2) & (lax.axis_index("slab") < SPECIAL)


def forward_first(given, table, out):
    blocks = [[given[pl.ds(t * 7 + i, SLAB, stride=14), :] for i in range(ROWS)] for t in range(2)]
    rest = [given[pl.ds(t * 7 + 6, SLAB, stride=14), :] for t in range(2)]
    lane = lanes(SLAB, 128)
    last = []
    for i in range(ROWS):
        value = jnp.where(lane < 64, turn(blocks[1][i], 64), turn(rest[i // 4], 64 - 32 * (i % 4)))
        last.append(jnp.where(lane < 32, turn(blocks[0][i], 32), value))
    low = dot(table[0:96, :], jnp.concatenate(blocks[0], axis=0))
    middle = dot(table[96:208, :], jnp.concatenate(blocks[1], axis=0))
    high = dot(table[208:288, :], jnp.concatenate(last, axis=0))
    parts = [low[i * 16 : i * 16 + 16] for i in range(6)] + [middle[i * 16 : i * 16 + 16] for i in range(6)]
    parts[5] = jnp.where(shared(128), middle[96:112], parts[5])
    parts[11] = parts[11] + high[0:16]
    parts += [high[i * 16 : i * 16 + 16] for i in range(1, 5)]
    lane = lanes(PENCIL, 128)
    for i in range(12):
        more = turn(parts[12 + i // 3], WIDE - 32 * (i % 3))
        out[pl.ds(i, PENCIL, stride=12), :] = jnp.where(lane < WIDE, parts[i], more)


def middle(given, sums, modes, forward, back, out, tiles, lines, rows):
    parts = [given[pl.ds(i, PENCIL, stride=12), :] for i in range(12)]
    parts += [gathered(parts[3 * i : 3 * i + 3], 32, WIDE) for i in range(4)]
    for slot in range(SLOTS):
        tiles[pl.ds(slot // 8 * 128 + slot % 8, PENCIL, stride=8), :] = parts[slot]
    lane = lanes(8, 128)
    masks = [((lane - COLS * m) & 127) < COLS for m in range(15)]
    for h in range(2):
        for t in range(2):
            turned = []
            for k in range(8):
                at = t * 128 + (8 * h + k) * 8
                turned.append(turn(tiles[at : at + 8, :], COLS * k))
            for u in range(2 * NB):
                value = turned[0]
                for k in range(1, 8):
                    value = jnp.where(masks[k + u], turned[k], value)
                at = u * SLOTS + t * 8
                lines[at : at + 8, h * 128 : h * 128 + 128] = turn(value, -COLS * u)
    spectrum = dot(lines[...], forward[...])
    lane = lanes(SLOTS, 128)
    own = modes[pl.ds(lax.axis_index("slab") * PENCIL + lax.axis_index("pencil"), 1), :]
    row = lax.broadcasted_iota(jnp.int32, (SLOTS, 128), 0)
    squared = jnp.sum(jnp.where(lane == row, own, 0.0), axis=1, keepdims=True)
    weight = jnp.sum(jnp.where(lane == row + SLOTS, own, 0.0), axis=1, keepdims=True)
    size = jnp.where(lane < CUT, lane, lane - CUT)
    squared = squared + (size * size).astype(jnp.float32)
    kinetic = jnp.where((lane < MODES) & (squared < float(CUT * CUT)), squared * (4.0 / CUT**2), 0.0)
    weight = weight * jnp.where(lane == 0, 1.0, jnp.where(lane == CUT, 0.0, 2.0)) * kinetic
    scaled, other = [], []
    for b in range(NB):
        value = spectrum[b * SLOTS : (b + 1) * SLOTS]
        scaled.append(value * weight)
        other.append(0.5 * kinetic * value + spectrum[(NB + b) * SLOTS : (NB + b + 1) * SLOTS])
    returned = dot(jnp.concatenate(scaled, axis=0), back[...])
    rows[...] = jnp.zeros_like(rows)
    for q, (a, b) in enumerate(PAIRS):
        term = scaled[a] * other[b] + scaled[b] * other[a]
        rows[q : q + 1, :] = jnp.sum(term, axis=0, keepdims=True)
    total = jnp.sum(rows[...], axis=1, keepdims=True) + jnp.sum(sums[...], axis=1, keepdims=True)
    note = jnp.sum(jnp.where(lane == row + WIDE, total, 0.0), axis=0, keepdims=True)
    for h in range(2):
        turned = []
        for c in range(2 * NB):
            at = c % NB * SLOTS + c // NB * 8
            turned.append(turn(returned[at : at + 8, h * 128 : h * 128 + 128], COLS * c))
        for k in range(8):
            p = 8 * h + k
            value = turned[0]
            for c in range(1, 2 * NB):
                value = jnp.where(masks[k + c], turned[c], value)
            tiles[p * 8 : p * 8 + 8, :] = turn(value, -COLS * k)
    parts = [tiles[pl.ds(i, PENCIL, stride=8), :] for i in range(8)]
    lane = lanes(PENCIL, 128)
    for i in range(6):
        more = turn(parts[6 + i // 3], WIDE - 32 * (i % 3))
        out[pl.ds(i, PENCIL, stride=7), :] = jnp.where(lane < WIDE, parts[i], more)
    out[pl.ds(6, PENCIL, stride=7), :] = jnp.broadcast_to(note, (PENCIL, 128))


def back_first(given, table, special, out):
    parts = [given[pl.ds(i, PENCIL, stride=7), :] for i in range(6)]
    note = jnp.sum(given[pl.ds(6, PENCIL, stride=7), :], axis=0, keepdims=True)
    parts += [gathered(parts[3 * i : 3 * i + 3], 32, WIDE) for i in range(2)]
    parts += parts
    lane = lanes(PENCIL, 128)
    row = lax.broadcasted_iota(jnp.int32, (PENCIL, 128), 0)
    inside = [lane < HALF, (lane >= HALF) & (lane < WIDE), lane >= WIDE, lane < 16]
    main, more = [], []
    empty = jnp.zeros((PENCIL, 128), jnp.float32)
    for slot in range(SLOTS):
        moved = turn(parts[slot], HALF)
        if slot < 6:
            value = jnp.where(inside[0], parts[slot], 0.0)
            if slot == 5:
                value = jnp.where(shared(128), jnp.where(inside[1], moved, 0.0), value)
        else:
            value = jnp.where(inside[1], moved if slot < 8 else parts[slot], 0.0)
        rest = empty
        if slot > 10:
            late = jnp.where(inside[2], moved, 0.0)
            rest = jnp.where(inside[3], moved, 0.0)
            if slot == 11:
                late, rest = jnp.where(row < SPLIT, value, late), jnp.where(row < SPLIT, 0.0, rest)
            value = late
        main.append(value)
        more.append(rest)
    given_all = jnp.concatenate([jnp.concatenate(main, axis=0), jnp.concatenate(more, axis=0)], axis=1)
    first = jnp.where(lax.axis_index("slab") < SPECIAL, special[...], table[:, 0:128])
    result = dot(jnp.concatenate([first, table[:, 128:256]], axis=1), given_all)
    pieces = []
    for i in range(ROWS):
        out[pl.ds(i, SLAB, stride=7), :] = result[i * SLAB : (i + 1) * SLAB, 0:128]
        pieces.append(result[i * SLAB : (i + 1) * SLAB, 128:256])
    out[pl.ds(6, SLAB, stride=7), :] = jnp.where(lanes(SLAB, 128) < WIDE, gathered(pieces, 16, 0), note)


def back_third(given, local, table, out, lines):
    rest = given[pl.ds(6, SLAB, stride=7), :]
    for i in range(ROWS):
        value = given[pl.ds(i, SLAB, stride=7), :]
        at = i * HALF
        lines[0:32, at : at + HALF] = value[:, :HALF]
        lines[32:64, at : at + HALF] = value[:, HALF:WIDE]
        lines[64:96, at : at + 32] = value[:, WIDE:128]
        lines[64:96, at + 32 : at + HALF] = rest[:, 16 * i : 16 * i + 16]
    kinetic_part = dot(lines[...], table[...], ((0,), (0,)))
    note = jnp.sum(rest, axis=0, keepdims=True) * (1.0 / CELLS)
    factor, inverse = {}, {}
    for q, (a, b) in enumerate(PAIRS):
        value = note[:, WIDE + q : WIDE + q + 1]
        for c in range(b):
            value = value - factor[a, c] * factor[b, c]
        if a == b:
            factor[a, a] = jnp.sqrt(value)
            inverse[a] = 1.0 / factor[a, a]
        else:
            factor[a, b] = value * inverse[b]
    for i in range(ROWS):
        done = []
        for a in range(NB):
            value = local[a, i] + kinetic_part[i * HALF + a * COLS : i * HALF + a * COLS + COLS]
            for b in range(a):
                value = value - factor[a, b] * done[b]
            value = value * inverse[a]
            done.append(value)
            out[i, :, a, :] = value


def f32(*shape):
    return jax.ShapeDtypeStruct(shape, jnp.float32)


def held(*shape):
    return pltpu.VMEM(shape, jnp.float32)


def call(body, kinds, outs, scratch=()):
    places = {"k": pltpu.VMEM, "h": pl.ANY}
    made = pl.pallas_call(
        body,
        out_shape=outs,
        in_specs=[pl.BlockSpec(memory_space=places[kind]) for kind in kinds],
        out_specs=jax.tree.map(lambda _: pl.BlockSpec(memory_space=pltpu.VMEM), outs),
        scratch_shapes=[pltpu.VMEM(shape, jnp.float32) if isinstance(shape, tuple) else shape for shape in scratch],
        name=body.__name__,
    )

    def run(*given):
        return made(*[pltpu.with_memory_space_constraint(x, places[kind]) for kind, x in zip(kinds, given)])

    return run


def trade(value, axis, number):
    rows = next(size for size in (8, 4, 2, 1) if value.shape[0] % (size * number) == 0)
    blocks = value.reshape(number, -1, rows, 128)
    return lax.all_to_all(blocks, axis, split_axis=0, concat_axis=0, tiled=True).reshape(value.shape)


def local_step(orbitals, potential, unlocked):
    third, first, first_back, special, second, second_back, modes = tables()
    outs = (held(SLAB * 14, 128), held(NB, ROWS, COLS, NG), held(16, NG))
    scratch = [pltpu.SMEM((NB,), jnp.int32)] + [(ROWS + 1, COLS, NB, 128), (ROWS + 1, COLS, NB, 64), (ROWS, COLS, NG), (MODES, NG), (ROWS * WIDE, NG)]
    made = call(forward_third, "hhhh", outs, scratch + [pltpu.SemaphoreType.DMA((2 * ROWS + 3,))])
    spectrum, local, sums = made(unlocked, orbitals.transpose(1, 2, 0, 3), potential, third)
    spectrum = trade(spectrum, "slab", SLAB)
    spectrum = trade(call(forward_first, "kk", held(PENCIL * 12, 128))(spectrum, first), "pencil", PENCIL)
    made = call(middle, "kkkkk", held(PENCIL * 7, 128), [(256, 128), (2 * NB * SLOTS, 256), (16, 128)])
    spectrum = trade(made(spectrum, sums, modes, second, second_back), "pencil", PENCIL)
    made = call(back_first, "kkk", held(SLAB * 7, 128))
    spectrum = trade(made(spectrum, first_back, special), "slab", SLAB)
    made = call(back_third, "kkk", f32(ROWS, COLS, NB, NG), [(MODES, ROWS * HALF)])
    return made(spectrum, local, third).transpose(2, 0, 1, 3)


def solution(mesh):
    in_specs = (P(None, "slab", "pencil", None), P("slab", "pencil", None), P())
    out_specs = P(None, "slab", "pencil", None)
    return jax.shard_map(local_step, mesh=mesh, in_specs=in_specs, out_specs=out_specs, check_vma=False)
```

```python
import functools

import jax
import jax.numpy as jnp
import numpy as np
from jax import lax
from jax.experimental import pallas as pl
from jax.experimental.pallas import tpu as pltpu
from jax.sharding import PartitionSpec as P

NG = 192
NB = 4
CUT = NG // 4
MODES = 2 * CUT
SLAB = 32
PENCIL = 16
ROWS = NG // SLAB
COLS = NG // PENCIL
CELLS = float(NG**3)
THIRDS = MODES // SLAB
FIRSTS = MODES // PENCIL
WIDE = 2 * NB * COLS
HALF = NB * COLS
PAIRS = [(a, b) for a in range(NB) for b in range(a + 1)]
highest = lax.Precision.HIGHEST

SLOTS = 16
SPLIT = 9
SPECIAL = 2


def basis():
    place = np.arange(NG)
    mode = np.arange(MODES)
    angle = 2.0 * np.pi / NG * ((mode[:, None] % CUT) * place[None, :] % NG)
    return np.where(mode[:, None] < CUT, np.cos(angle), np.sin(angle))


def thirds(rank):
    return [(start + way * (rank // 2)) + CUT * (rank % 2) for start, way in ((15, -1), (16, 1), (32, 1))]


def below(limit):
    return [m for m in range(MODES) if m % CUT < limit and m != CUT]


def slots():
    kinds = [[0] * PENCIL] * 6 + [[1] * PENCIL] * 5 + [[1] * SPLIT + [2] * (PENCIL - SPLIT)] + [[2] * PENCIL] * 4
    queues = [below(47) + [CUT, 47, 95], below(45), below(36)]
    firsts = [[queues[kinds[slot][p]].pop(0) for p in range(PENCIL)] for slot in range(SLOTS)]
    assert not any(queues)
    return np.array(kinds), np.array(firsts), {PENCIL - 2: 45, PENCIL - 1: 93}


def mode_table():
    kinds, firsts, others = slots()
    table = np.zeros((SLAB, PENCIL, 128))
    weight = np.where(np.arange(MODES) == 0, 1.0, np.where(np.arange(MODES) == CUT, 0.0, 2.0))
    for rank in range(SLAB):
        for p in range(PENCIL):
            for slot in range(SLOTS):
                kind, first = kinds[slot, p], firsts[slot, p]
                if rank < SPECIAL and slot == 5 and p in others:
                    kind, first = 1, others[p]
                third = thirds(rank)[kind]
                table[rank, p, slot] = (third % CUT) ** 2 + (first % CUT) ** 2
                table[rank, p, SLOTS + slot] = weight[third] * weight[first] / CELLS
    return np.concatenate([table.reshape(SLAB * PENCIL, 128), np.zeros((8, 128))])


def tables():
    real = basis()
    third = np.concatenate([real[[thirds(rank)[t] for rank in range(SLAB)]] for t in range(THIRDS)])
    kinds, firsts, others = slots()
    lines = real.reshape(MODES, SLAB, ROWS).transpose(0, 2, 1).reshape(MODES, NG)
    rows = [np.where((kinds == t)[:, :, None], lines[firsts], 0.0) for t in range(THIRDS)]
    extra = np.zeros((PENCIL, NG))
    for p, m in others.items():
        extra[p] = lines[m]
    parts = [rows[0][0:6], np.concatenate([rows[1][6:12], extra[None]]), rows[2][11:16]]
    parts = [part.reshape(-1, NG) for part in parts]
    second = np.zeros((128, 2, 128))
    second[:MODES, :, : NG // 2] = real.reshape(MODES, 2, NG // 2)
    second = second.reshape(128, 256)
    every = lines[firsts]
    back = every.reshape(-1, NG).T.copy()
    for p, m in others.items():
        every[5, p] = lines[m]
    special = every.reshape(-1, NG).T[:, 0:128]
    made = [third, np.concatenate(parts), back, special, second.T, second, mode_table()]
    return [np.ascontiguousarray(t, dtype=np.float32) for t in made]


def dot(a, b, dims=((1,), (0,))):
    return lax.dot_general(a, b, (dims, ((), ())), precision=highest, preferred_element_type=jnp.float32)


def lanes(*shape):
    return lax.broadcasted_iota(jnp.int32, shape, len(shape) - 1)


def turn(value, by):
    by = by % 128
    return pltpu.roll(value, by, 1) if by else value


def gathered(pieces, width, start):
    lane = lanes(*pieces[0].shape)
    result = jnp.zeros(pieces[0].shape, jnp.float32)
    for k, piece in enumerate(pieces):
        here = (lane >= k * width) & (lane < k * width + width)
        result = jnp.where(here, turn(piece, k * width - start), result)
    return result


def forward_third(flags, orbitals, potential, table, out, local, sums, kind, low, high, field, made, lines, ready):
    copies = [pltpu.make_async_copy(flags, kind, ready.at[0]), pltpu.make_async_copy(potential, field, ready.at[1])]
    for i in range(ROWS):
        copies.append(pltpu.make_async_copy(orbitals.at[i, :, :, 0:128], low.at[i], ready.at[2 + 2 * i]))
        copies.append(pltpu.make_async_copy(orbitals.at[i, :, :, 128:NG], high.at[i], ready.at[3 + 2 * i]))
    copies.append(pltpu.make_async_copy(table, made, ready.at[2 + 2 * ROWS]))
    low, high = low.reshape((ROWS + 1) * COLS * NB, 128), high.reshape((ROWS + 1) * COLS * NB, 64)
    for copy in copies:
        copy.start()
    copies[0].wait()
    copies[1].wait()
    totals = [None] * len(PAIRS)
    for i in range(ROWS):
        copies[2 + 2 * i].wait()
        copies[3 + 2 * i].wait()
        shifted = (field[i] - 1.0) * (1.0 / 1.5)
        own = []
        for b in range(NB):
            base = i * WIDE + b * COLS
            parts = [ref[pl.ds(i * WIDE // 2 + b, COLS, stride=NB), :] for ref in (low, high)]
            value = jnp.concatenate([parts[0], parts[1]], axis=1)
            kept = jnp.where(kind[b] == 1, value * shifted, value)
            lines[base : base + COLS, :] = value
            lines[base + HALF : base + HALF + COLS, :] = kept
            local[b, i] = kept
            own.append(kept)
        for q, (a, b) in enumerate(PAIRS):
            term = own[a] * own[b]
            totals[q] = term if totals[q] is None else totals[q] + term
    copies[-1].wait()
    whole = lanes(SLAB, 128)
    last = []
    lane = lanes(MODES, 128)
    scale = jnp.ones((MODES, 128), jnp.float32)
    for b in range(NB):
        alpha = jnp.where(kind[b] == 1, 1.0 / 1.5, 0.0)
        scale = jnp.where((lane >= b * COLS) & (lane < (b + 1) * COLS), alpha, scale)
    for i in range(ROWS):
        if i % 2 == 0:
            spectrum = dot(made[...], lines[i * WIDE : i * WIDE + 2 * WIDE, :], ((1,), (1,)))
            result = spectrum[:, :128]
        else:
            more = jnp.concatenate([spectrum[:, 128:], jnp.zeros((MODES, 64), jnp.float32)], axis=1)
            result = jnp.where(lanes(MODES, 128) < 32, turn(spectrum[:, :128], 32), turn(more, 32))
        result = result * scale
        parts = [result[t * 32 : t * 32 + 32] for t in range(THIRDS)]
        for t in range(2):
            extra = turn(parts[2], WIDE - 32 * t)
            out[pl.ds(t * 7 + i, SLAB, stride=14), :] = jnp.where(whole < WIDE, parts[t], extra)
        last.append(parts[2])
    sums[...] = jnp.zeros_like(sums)
    for q in range(len(PAIRS)):
        sums[q : q + 1, :] = jnp.sum(totals[q], axis=0, keepdims=True)
    for t in range(2):
        out[pl.ds(t * 7 + 6, SLAB, stride=14), :] = gathered(last[t * 4 : t * 4 + 4], 32, 64)


def shared(number):
    row = lax.broadcasted_iota(jnp.int32, (PENCIL, number), 0)
    return (row >= PENCIL - 2) & (lax.axis_index("slab") < SPECIAL)


def forward_first(given, table, out):
    blocks = [[given[pl.ds(t * 7 + i, SLAB, stride=14), :] for i in range(ROWS)] for t in range(2)]
    rest = [given[pl.ds(t * 7 + 6, SLAB, stride=14), :] for t in range(2)]
    lane = lanes(SLAB, 128)
    last = []
    for i in range(ROWS):
        value = jnp.where(lane < 64, turn(blocks[1][i], 64), turn(rest[i // 4], 64 - 32 * (i % 4)))
        last.append(jnp.where(lane < 32, turn(blocks[0][i], 32), value))
    low = dot(table[0:96, :], jnp.concatenate(blocks[0], axis=0))
    middle = dot(table[96:208, :], jnp.concatenate(blocks[1], axis=0))
    high = dot(table[208:288, :], jnp.concatenate(last, axis=0))
    parts = [low[i * 16 : i * 16 + 16] for i in range(6)] + [middle[i * 16 : i * 16 + 16] for i in range(6)]
    parts[5] = jnp.where(shared(128), middle[96:112], parts[5])
    parts[11] = parts[11] + high[0:16]
    parts += [high[i * 16 : i * 16 + 16] for i in range(1, 5)]
    lane = lanes(PENCIL, 128)
    for i in range(12):
        more = turn(parts[12 + i // 3], WIDE - 32 * (i % 3))
        out[pl.ds(i, PENCIL, stride=12), :] = jnp.where(lane < WIDE, parts[i], more)


def middle(given, sums, modes, forward, back, out, tiles, lines, rows):
    parts = [given[pl.ds(i, PENCIL, stride=12), :] for i in range(12)]
    parts += [gathered(parts[3 * i : 3 * i + 3], 32, WIDE) for i in range(4)]
    for slot in range(SLOTS):
        tiles[pl.ds(slot // 8 * 128 + slot % 8, PENCIL, stride=8), :] = parts[slot]
    lane = lanes(8, 128)
    masks = [((lane - COLS * m) & 127) < COLS for m in range(15)]
    for h in range(2):
        for t in range(2):
            turned = []
            for k in range(8):
                at = t * 128 + (8 * h + k) * 8
                turned.append(turn(tiles[at : at + 8, :], COLS * k))
            for u in range(2 * NB):
                value = turned[0]
                for k in range(1, 8):
                    value = jnp.where(masks[k + u], turned[k], value)
                at = u * SLOTS + t * 8
                lines[at : at + 8, h * 128 : h * 128 + 128] = turn(value, -COLS * u)
    spectrum = dot(lines[...], forward[...])
    lane = lanes(SLOTS, 128)
    own = modes[pl.ds(lax.axis_index("slab") * PENCIL + lax.axis_index("pencil"), 1), :]
    row = lax.broadcasted_iota(jnp.int32, (SLOTS, 128), 0)
    squared = jnp.sum(jnp.where(lane == row, own, 0.0), axis=1, keepdims=True)
    weight = jnp.sum(jnp.where(lane == row + SLOTS, own, 0.0), axis=1, keepdims=True)
    size = jnp.where(lane < CUT, lane, lane - CUT)
    squared = squared + (size * size).astype(jnp.float32)
    kinetic = jnp.where((lane < MODES) & (squared < float(CUT * CUT)), squared * (4.0 / CUT**2), 0.0)
    weight = weight * jnp.where(lane == 0, 1.0, jnp.where(lane == CUT, 0.0, 2.0)) * kinetic
    scaled, other = [], []
    for b in range(NB):
        value = spectrum[b * SLOTS : (b + 1) * SLOTS]
        scaled.append(value * weight)
        other.append(0.5 * kinetic * value + spectrum[(NB + b) * SLOTS : (NB + b + 1) * SLOTS])
    returned = dot(jnp.concatenate(scaled, axis=0), back[...])
    rows[...] = jnp.zeros_like(rows)
    for q, (a, b) in enumerate(PAIRS):
        term = scaled[a] * other[b] + scaled[b] * other[a]
        rows[q : q + 1, :] = jnp.sum(term, axis=0, keepdims=True)
    total = jnp.sum(rows[...], axis=1, keepdims=True) + jnp.sum(sums[...], axis=1, keepdims=True)
    note = jnp.sum(jnp.where(lane == row + WIDE, total, 0.0), axis=0, keepdims=True)
    for h in range(2):
        turned = []
        for c in range(2 * NB):
            at = c % NB * SLOTS + c // NB * 8
            turned.append(turn(returned[at : at + 8, h * 128 : h * 128 + 128], COLS * c))
        for k in range(8):
            p = 8 * h + k
            value = turned[0]
            for c in range(1, 2 * NB):
                value = jnp.where(masks[k + c], turned[c], value)
            tiles[p * 8 : p * 8 + 8, :] = turn(value, -COLS * k)
    parts = [tiles[pl.ds(i, PENCIL, stride=8), :] for i in range(8)]
    lane = lanes(PENCIL, 128)
    for i in range(6):
        more = turn(parts[6 + i // 3], WIDE - 32 * (i % 3))
        out[pl.ds(i, PENCIL, stride=7), :] = jnp.where(lane < WIDE, parts[i], more)
    out[pl.ds(6, PENCIL, stride=7), :] = jnp.broadcast_to(note, (PENCIL, 128))


def back_first(given, table, special, out):
    parts = [given[pl.ds(i, PENCIL, stride=7), :] for i in range(6)]
    note = jnp.sum(given[pl.ds(6, PENCIL, stride=7), :], axis=0, keepdims=True)
    parts += [gathered(parts[3 * i : 3 * i + 3], 32, WIDE) for i in range(2)]
    parts += parts
    lane = lanes(PENCIL, 128)
    row = lax.broadcasted_iota(jnp.int32, (PENCIL, 128), 0)
    inside = [lane < HALF, (lane >= HALF) & (lane < WIDE), lane >= WIDE, lane < 16]
    main, more = [], []
    empty = jnp.zeros((PENCIL, 128), jnp.float32)
    for slot in range(SLOTS):
        moved = turn(parts[slot], HALF)
        if slot < 6:
            value = jnp.where(inside[0], parts[slot], 0.0)
            if slot == 5:
                value = jnp.where(shared(128), jnp.where(inside[1], moved, 0.0), value)
        else:
            value = jnp.where(inside[1], moved if slot < 8 else parts[slot], 0.0)
        rest = empty
        if slot > 10:
            late = jnp.where(inside[2], moved, 0.0)
            rest = jnp.where(inside[3], moved, 0.0)
            if slot == 11:
                late, rest = jnp.where(row < SPLIT, value, late), jnp.where(row < SPLIT, 0.0, rest)
            value = late
        main.append(value)
        more.append(rest)
    given_all = jnp.concatenate([jnp.concatenate(main, axis=0), jnp.concatenate(more, axis=0)], axis=1)
    first = jnp.where(lax.axis_index("slab") < SPECIAL, special[...], table[:, 0:128])
    result = dot(jnp.concatenate([first, table[:, 128:256]], axis=1), given_all)
    pieces = []
    for i in range(ROWS):
        out[pl.ds(i, SLAB, stride=7), :] = result[i * SLAB : (i + 1) * SLAB, 0:128]
        pieces.append(result[i * SLAB : (i + 1) * SLAB, 128:256])
    out[pl.ds(6, SLAB, stride=7), :] = jnp.where(lanes(SLAB, 128) < WIDE, gathered(pieces, 16, 0), note)


def back_third(given, local, table, out, lines):
    rest = given[pl.ds(6, SLAB, stride=7), :]
    for i in range(ROWS):
        value = given[pl.ds(i, SLAB, stride=7), :]
        at = i * HALF
        lines[0:32, at : at + HALF] = value[:, :HALF]
        lines[32:64, at : at + HALF] = value[:, HALF:WIDE]
        lines[64:96, at : at + 32] = value[:, WIDE:128]
        lines[64:96, at + 32 : at + HALF] = rest[:, 16 * i : 16 * i + 16]
    kinetic_part = dot(lines[...], table[...], ((0,), (0,)))
    note = jnp.sum(rest, axis=0, keepdims=True) * (1.0 / CELLS)
    factor, inverse = {}, {}
    for q, (a, b) in enumerate(PAIRS):
        value = note[:, WIDE + q : WIDE + q + 1]
        for c in range(b):
            value = value - factor[a, c] * factor[b, c]
        if a == b:
            factor[a, a] = jnp.sqrt(value)
            inverse[a] = 1.0 / factor[a, a]
        else:
            factor[a, b] = value * inverse[b]
    for i in range(ROWS):
        done = []
        for a in range(NB):
            value = local[a, i] + kinetic_part[i * HALF + a * COLS : i * HALF + a * COLS + COLS]
            for b in range(a):
                value = value - factor[a, b] * done[b]
            value = value * inverse[a]
            done.append(value)
            out[i, :, a, :] = value


def f32(*shape):
    return jax.ShapeDtypeStruct(shape, jnp.float32)


def held(*shape):
    return pltpu.VMEM(shape, jnp.float32)


def call(body, kinds, outs, scratch=()):
    places = {"k": pltpu.VMEM, "h": pl.ANY}
    made = pl.pallas_call(
        body,
        out_shape=outs,
        in_specs=[pl.BlockSpec(memory_space=places[kind]) for kind in kinds],
        out_specs=jax.tree.map(lambda _: pl.BlockSpec(memory_space=pltpu.VMEM), outs),
        scratch_shapes=[pltpu.VMEM(shape, jnp.float32) if isinstance(shape, tuple) else shape for shape in scratch],
        name=body.__name__,
    )

    def run(*given):
        return made(*[pltpu.with_memory_space_constraint(x, places[kind]) for kind, x in zip(kinds, given)])

    return run


def trade(value, axis, number):
    rows = next(size for size in (1,) if value.shape[0] % (size * number) == 0)
    blocks = value.reshape(number, -1, rows, 128)
    return lax.all_to_all(blocks, axis, split_axis=0, concat_axis=0, tiled=True).reshape(value.shape)


def local_step(orbitals, potential, unlocked):
    third, first, first_back, special, second, second_back, modes = tables()
    outs = (held(SLAB * 14, 128), held(NB, ROWS, COLS, NG), held(16, NG))
    scratch = [pltpu.SMEM((NB,), jnp.int32)] + [(ROWS + 1, COLS, NB, 128), (ROWS + 1, COLS, NB, 64), (ROWS, COLS, NG), (MODES, NG), (ROWS * WIDE, NG)]
    made = call(forward_third, "hhhh", outs, scratch + [pltpu.SemaphoreType.DMA((2 * ROWS + 3,))])
    spectrum, local, sums = made(unlocked, orbitals.transpose(1, 2, 0, 3), potential, third)
    spectrum = trade(spectrum, "slab", SLAB)
    spectrum = trade(call(forward_first, "kk", held(PENCIL * 12, 128))(spectrum, first), "pencil", PENCIL)
    made = call(middle, "kkkkk", held(PENCIL * 7, 128), [(256, 128), (2 * NB * SLOTS, 256), (16, 128)])
    spectrum = trade(made(spectrum, sums, modes, second, second_back), "pencil", PENCIL)
    made = call(back_first, "kkk", held(SLAB * 7, 128))
    spectrum = trade(made(spectrum, first_back, special), "slab", SLAB)
    made = call(back_third, "kkk", f32(ROWS, COLS, NB, NG), [(MODES, ROWS * HALF)])
    return made(spectrum, local, third).transpose(2, 0, 1, 3)


def solution(mesh):
    in_specs = (P(None, "slab", "pencil", None), P("slab", "pencil", None), P())
    out_specs = P(None, "slab", "pencil", None)
    return jax.shard_map(local_step, mesh=mesh, in_specs=in_specs, out_specs=out_specs, check_vma=False)
```

```python
import functools

import jax
import jax.numpy as jnp
import numpy as np
from jax import lax
from jax.experimental import pallas as pl
from jax.experimental.pallas import tpu as pltpu
from jax.sharding import PartitionSpec as P

NG = 192
NB = 4
CUT = NG // 4
MODES = 2 * CUT
SLAB = 32
PENCIL = 16
ROWS = NG // SLAB
COLS = NG // PENCIL
CELLS = float(NG**3)
THIRDS = MODES // SLAB
FIRSTS = MODES // PENCIL
WIDE = 2 * NB * COLS
HALF = NB * COLS
PAIRS = [(a, b) for a in range(NB) for b in range(a + 1)]
highest = lax.Precision.HIGHEST

SLOTS = 16
SPLIT = 9
SPECIAL = 2


def basis():
    place = np.arange(NG)
    mode = np.arange(MODES)
    angle = 2.0 * np.pi / NG * ((mode[:, None] % CUT) * place[None, :] % NG)
    return np.where(mode[:, None] < CUT, np.cos(angle), np.sin(angle))


def thirds(rank):
    return [(start + way * (rank // 2)) + CUT * (rank % 2) for start, way in ((15, -1), (16, 1), (32, 1))]


def below(limit):
    return [m for m in range(MODES) if m % CUT < limit and m != CUT]


def slots():
    kinds = [[0] * PENCIL] * 6 + [[1] * PENCIL] * 5 + [[1] * SPLIT + [2] * (PENCIL - SPLIT)] + [[2] * PENCIL] * 4
    queues = [below(47) + [CUT, 47, 95], below(45), below(36)]
    firsts = [[queues[kinds[slot][p]].pop(0) for p in range(PENCIL)] for slot in range(SLOTS)]
    assert not any(queues)
    return np.array(kinds), np.array(firsts), {PENCIL - 2: 45, PENCIL - 1: 93}


def mode_table():
    kinds, firsts, others = slots()
    table = np.zeros((SLAB, PENCIL, 128))
    weight = np.where(np.arange(MODES) == 0, 1.0, np.where(np.arange(MODES) == CUT, 0.0, 2.0))
    for rank in range(SLAB):
        for p in range(PENCIL):
            for slot in range(SLOTS):
                kind, first = kinds[slot, p], firsts[slot, p]
                if rank < SPECIAL and slot == 5 and p in others:
                    kind, first = 1, others[p]
                third = thirds(rank)[kind]
                table[rank, p, slot] = (third % CUT) ** 2 + (first % CUT) ** 2
                table[rank, p, SLOTS + slot] = weight[third] * weight[first] / CELLS
    return np.concatenate([table.reshape(SLAB * PENCIL, 128), np.zeros((8, 128))])


def tables():
    real = basis()
    third = np.concatenate([real[[thirds(rank)[t] for rank in range(SLAB)]] for t in range(THIRDS)])
    kinds, firsts, others = slots()
    lines = real.reshape(MODES, SLAB, ROWS).transpose(0, 2, 1).reshape(MODES, NG)
    rows = [np.where((kinds == t)[:, :, None], lines[firsts], 0.0) for t in range(THIRDS)]
    extra = np.zeros((PENCIL, NG))
    for p, m in others.items():
        extra[p] = lines[m]
    parts = [rows[0][0:6], np.concatenate([rows[1][6:12], extra[None]]), rows[2][11:16]]
    parts = [part.reshape(-1, NG) for part in parts]
    second = np.zeros((128, 2, 128))
    second[:MODES, :, : NG // 2] = real.reshape(MODES, 2, NG // 2)
    second = second.reshape(128, 256)
    every = lines[firsts]
    back = every.reshape(-1, NG).T.copy()
    for p, m in others.items():
        every[5, p] = lines[m]
    special = every.reshape(-1, NG).T[:, 0:128]
    made = [third, np.concatenate(parts), back, special, second.T, second, mode_table()]
    return [np.ascontiguousarray(t, dtype=np.float32) for t in made]


def dot(a, b, dims=((1,), (0,))):
    return lax.dot_general(a, b, (dims, ((), ())), precision=highest, preferred_element_type=jnp.float32)


def lanes(*shape):
    return lax.broadcasted_iota(jnp.int32, shape, len(shape) - 1)


def turn(value, by):
    by = by % 128
    return pltpu.roll(value, by, 1) if by else value


def gathered(pieces, width, start):
    lane = lanes(*pieces[0].shape)
    result = jnp.zeros(pieces[0].shape, jnp.float32)
    for k, piece in enumerate(pieces):
        here = (lane >= k * width) & (lane < k * width + width)
        result = jnp.where(here, turn(piece, k * width - start), result)
    return result


def forward_third(flags, orbitals, potential, table, out, local, sums, kind, low, high, field, made, lines, ready):
    copies = [pltpu.make_async_copy(flags, kind, ready.at[0]), pltpu.make_async_copy(potential, field, ready.at[1])]
    for i in range(0, ROWS, 2):
        copies.append(pltpu.make_async_copy(orbitals.at[i : i + 2, :, :, 0:128], low.at[i : i + 2], ready.at[2 + 2 * i]))
        copies.append(pltpu.make_async_copy(orbitals.at[i : i + 2, :, :, 128:NG], high.at[i : i + 2], ready.at[3 + 2 * i]))
    copies.append(pltpu.make_async_copy(table, made, ready.at[2 + 2 * ROWS]))
    low, high = low.reshape((ROWS + 1) * COLS * NB, 128), high.reshape((ROWS + 1) * COLS * NB, 64)
    for copy in copies:
        copy.start()
    copies[0].wait()
    copies[1].wait()
    totals = [None] * len(PAIRS)
    for i in range(ROWS):
        if i % 2 == 0:
            copies[2 + i // 2 * 2].wait()
            copies[3 + i // 2 * 2].wait()
        shifted = (field[i] - 1.0) * (1.0 / 1.5)
        own = []
        for b in range(NB):
            base = i * WIDE + b * COLS
            parts = [ref[pl.ds(i * WIDE // 2 + b, COLS, stride=NB), :] for ref in (low, high)]
            value = jnp.concatenate([parts[0], parts[1]], axis=1)
            kept = jnp.where(kind[b] == 1, value * shifted, value)
            lines[base : base + COLS, :] = value
            lines[base + HALF : base + HALF + COLS, :] = kept
            local[b, i] = kept
            own.append(kept)
        for q, (a, b) in enumerate(PAIRS):
            term = own[a] * own[b]
            totals[q] = term if totals[q] is None else totals[q] + term
    copies[-1].wait()
    whole = lanes(SLAB, 128)
    last = []
    lane = lanes(MODES, 128)
    scale = jnp.ones((MODES, 128), jnp.float32)
    for b in range(NB):
        alpha = jnp.where(kind[b] == 1, 1.0 / 1.5, 0.0)
        scale = jnp.where((lane >= b * COLS) & (lane < (b + 1) * COLS), alpha, scale)
    for i in range(ROWS):
        if i % 2 == 0:
            spectrum = dot(made[...], lines[i * WIDE : i * WIDE + 2 * WIDE, :], ((1,), (1,)))
            result = spectrum[:, :128]
        else:
            more = jnp.concatenate([spectrum[:, 128:], jnp.zeros((MODES, 64), jnp.float32)], axis=1)
            result = jnp.where(lanes(MODES, 128) < 32, turn(spectrum[:, :128], 32), turn(more, 32))
        result = result * scale
        parts = [result[t * 32 : t * 32 + 32] for t in range(THIRDS)]
        for t in range(2):
            extra = turn(parts[2], WIDE - 32 * t)
            out[pl.ds(t * 7 + i, SLAB, stride=14), :] = jnp.where(whole < WIDE, parts[t], extra)
        last.append(parts[2])
    sums[...] = jnp.zeros_like(sums)
    for q in range(len(PAIRS)):
        sums[q : q + 1, :] = jnp.sum(totals[q], axis=0, keepdims=True)
    for t in range(2):
        out[pl.ds(t * 7 + 6, SLAB, stride=14), :] = gathered(last[t * 4 : t * 4 + 4], 32, 64)


def shared(number):
    row = lax.broadcasted_iota(jnp.int32, (PENCIL, number), 0)
    return (row >= PENCIL - 2) & (lax.axis_index("slab") < SPECIAL)


def forward_first(given, table, out):
    blocks = [[given[pl.ds(t * 7 + i, SLAB, stride=14), :] for i in range(ROWS)] for t in range(2)]
    rest = [given[pl.ds(t * 7 + 6, SLAB, stride=14), :] for t in range(2)]
    lane = lanes(SLAB, 128)
    last = []
    for i in range(ROWS):
        value = jnp.where(lane < 64, turn(blocks[1][i], 64), turn(rest[i // 4], 64 - 32 * (i % 4)))
        last.append(jnp.where(lane < 32, turn(blocks[0][i], 32), value))
    low = dot(table[0:96, :], jnp.concatenate(blocks[0], axis=0))
    middle = dot(table[96:208, :], jnp.concatenate(blocks[1], axis=0))
    high = dot(table[208:288, :], jnp.concatenate(last, axis=0))
    parts = [low[i * 16 : i * 16 + 16] for i in range(6)] + [middle[i * 16 : i * 16 + 16] for i in range(6)]
    parts[5] = jnp.where(shared(128), middle[96:112], parts[5])
    parts[11] = parts[11] + high[0:16]
    parts += [high[i * 16 : i * 16 + 16] for i in range(1, 5)]
    lane = lanes(PENCIL, 128)
    for i in range(12):
        more = turn(parts[12 + i // 3], WIDE - 32 * (i % 3))
        out[pl.ds(i, PENCIL, stride=12), :] = jnp.where(lane < WIDE, parts[i], more)


def middle(given, sums, modes, forward, back, out, tiles, lines, rows):
    parts = [given[pl.ds(i, PENCIL, stride=12), :] for i in range(12)]
    parts += [gathered(parts[3 * i : 3 * i + 3], 32, WIDE) for i in range(4)]
    for slot in range(SLOTS):
        tiles[pl.ds(slot // 8 * 128 + slot % 8, PENCIL, stride=8), :] = parts[slot]
    lane = lanes(8, 128)
    masks = [((lane - COLS * m) & 127) < COLS for m in range(15)]
    for h in range(2):
        for t in range(2):
            turned = []
            for k in range(8):
                at = t * 128 + (8 * h + k) * 8
                turned.append(turn(tiles[at : at + 8, :], COLS * k))
            for u in range(2 * NB):
                value = turned[0]
                for k in range(1, 8):
                    value = jnp.where(masks[k + u], turned[k], value)
                at = u * SLOTS + t * 8
                lines[at : at + 8, h * 128 : h * 128 + 128] = turn(value, -COLS * u)
    spectrum = dot(lines[...], forward[...])
    lane = lanes(SLOTS, 128)
    own = modes[pl.ds(lax.axis_index("slab") * PENCIL + lax.axis_index("pencil"), 1), :]
    row = lax.broadcasted_iota(jnp.int32, (SLOTS, 128), 0)
    squared = jnp.sum(jnp.where(lane == row, own, 0.0), axis=1, keepdims=True)
    weight = jnp.sum(jnp.where(lane == row + SLOTS, own, 0.0), axis=1, keepdims=True)
    size = jnp.where(lane < CUT, lane, lane - CUT)
    squared = squared + (size * size).astype(jnp.float32)
    kinetic = jnp.where((lane < MODES) & (squared < float(CUT * CUT)), squared * (4.0 / CUT**2), 0.0)
    weight = weight * jnp.where(lane == 0, 1.0, jnp.where(lane == CUT, 0.0, 2.0)) * kinetic
    scaled, other = [], []
    for b in range(NB):
        value = spectrum[b * SLOTS : (b + 1) * SLOTS]
        scaled.append(value * weight)
        other.append(0.5 * kinetic * value + spectrum[(NB + b) * SLOTS : (NB + b + 1) * SLOTS])
    returned = dot(jnp.concatenate(scaled, axis=0), back[...])
    rows[...] = jnp.zeros_like(rows)
    for q, (a, b) in enumerate(PAIRS):
        term = scaled[a] * other[b] + scaled[b] * other[a]
        rows[q : q + 1, :] = jnp.sum(term, axis=0, keepdims=True)
    total = jnp.sum(rows[...], axis=1, keepdims=True) + jnp.sum(sums[...], axis=1, keepdims=True)
    note = jnp.sum(jnp.where(lane == row + WIDE, total, 0.0), axis=0, keepdims=True)
    for h in range(2):
        turned = []
        for c in range(2 * NB):
            at = c % NB * SLOTS + c // NB * 8
            turned.append(turn(returned[at : at + 8, h * 128 : h * 128 + 128], COLS * c))
        for k in range(8):
            p = 8 * h + k
            value = turned[0]
            for c in range(1, 2 * NB):
                value = jnp.where(masks[k + c], turned[c], value)
            tiles[p * 8 : p * 8 + 8, :] = turn(value, -COLS * k)
    parts = [tiles[pl.ds(i, PENCIL, stride=8), :] for i in range(8)]
    lane = lanes(PENCIL, 128)
    for i in range(6):
        more = turn(parts[6 + i // 3], WIDE - 32 * (i % 3))
        out[pl.ds(i, PENCIL, stride=7), :] = jnp.where(lane < WIDE, parts[i], more)
    out[pl.ds(6, PENCIL, stride=7), :] = jnp.broadcast_to(note, (PENCIL, 128))


def back_first(given, table, special, out):
    parts = [given[pl.ds(i, PENCIL, stride=7), :] for i in range(6)]
    note = jnp.sum(given[pl.ds(6, PENCIL, stride=7), :], axis=0, keepdims=True)
    parts += [gathered(parts[3 * i : 3 * i + 3], 32, WIDE) for i in range(2)]
    parts += parts
    lane = lanes(PENCIL, 128)
    row = lax.broadcasted_iota(jnp.int32, (PENCIL, 128), 0)
    inside = [lane < HALF, (lane >= HALF) & (lane < WIDE), lane >= WIDE, lane < 16]
    main, more = [], []
    empty = jnp.zeros((PENCIL, 128), jnp.float32)
    for slot in range(SLOTS):
        moved = turn(parts[slot], HALF)
        if slot < 6:
            value = jnp.where(inside[0], parts[slot], 0.0)
            if slot == 5:
                value = jnp.where(shared(128), jnp.where(inside[1], moved, 0.0), value)
        else:
            value = jnp.where(inside[1], moved if slot < 8 else parts[slot], 0.0)
        rest = empty
        if slot > 10:
            late = jnp.where(inside[2], moved, 0.0)
            rest = jnp.where(inside[3], moved, 0.0)
            if slot == 11:
                late, rest = jnp.where(row < SPLIT, value, late), jnp.where(row < SPLIT, 0.0, rest)
            value = late
        main.append(value)
        more.append(rest)
    given_all = jnp.concatenate([jnp.concatenate(main, axis=0), jnp.concatenate(more, axis=0)], axis=1)
    first = jnp.where(lax.axis_index("slab") < SPECIAL, special[...], table[:, 0:128])
    result = dot(jnp.concatenate([first, table[:, 128:256]], axis=1), given_all)
    pieces = []
    for i in range(ROWS):
        out[pl.ds(i, SLAB, stride=7), :] = result[i * SLAB : (i + 1) * SLAB, 0:128]
        pieces.append(result[i * SLAB : (i + 1) * SLAB, 128:256])
    out[pl.ds(6, SLAB, stride=7), :] = jnp.where(lanes(SLAB, 128) < WIDE, gathered(pieces, 16, 0), note)


def back_third(given, local, table, out, lines):
    rest = given[pl.ds(6, SLAB, stride=7), :]
    for i in range(ROWS):
        value = given[pl.ds(i, SLAB, stride=7), :]
        at = i * HALF
        lines[0:32, at : at + HALF] = value[:, :HALF]
        lines[32:64, at : at + HALF] = value[:, HALF:WIDE]
        lines[64:96, at : at + 32] = value[:, WIDE:128]
        lines[64:96, at + 32 : at + HALF] = rest[:, 16 * i : 16 * i + 16]
    kinetic_part = dot(lines[...], table[...], ((0,), (0,)))
    note = jnp.sum(rest, axis=0, keepdims=True) * (1.0 / CELLS)
    factor, inverse = {}, {}
    for q, (a, b) in enumerate(PAIRS):
        value = note[:, WIDE + q : WIDE + q + 1]
        for c in range(b):
            value = value - factor[a, c] * factor[b, c]
        if a == b:
            factor[a, a] = jnp.sqrt(value)
            inverse[a] = 1.0 / factor[a, a]
        else:
            factor[a, b] = value * inverse[b]
    for i in range(ROWS):
        done = []
        for a in range(NB):
            value = local[a, i] + kinetic_part[i * HALF + a * COLS : i * HALF + a * COLS + COLS]
            for b in range(a):
                value = value - factor[a, b] * done[b]
            value = value * inverse[a]
            done.append(value)
            out[i, :, a, :] = value


def f32(*shape):
    return jax.ShapeDtypeStruct(shape, jnp.float32)


def held(*shape):
    return pltpu.VMEM(shape, jnp.float32)


def call(body, kinds, outs, scratch=()):
    places = {"k": pltpu.VMEM, "h": pl.ANY}
    made = pl.pallas_call(
        body,
        out_shape=outs,
        in_specs=[pl.BlockSpec(memory_space=places[kind]) for kind in kinds],
        out_specs=jax.tree.map(lambda _: pl.BlockSpec(memory_space=pltpu.VMEM), outs),
        scratch_shapes=[pltpu.VMEM(shape, jnp.float32) if isinstance(shape, tuple) else shape for shape in scratch],
        name=body.__name__,
    )

    def run(*given):
        return made(*[pltpu.with_memory_space_constraint(x, places[kind]) for kind, x in zip(kinds, given)])

    return run


def trade(value, axis, number):
    rows = next(size for size in (8, 4, 2, 1) if value.shape[0] % (size * number) == 0)
    blocks = value.reshape(number, -1, rows, 128)
    return lax.all_to_all(blocks, axis, split_axis=0, concat_axis=0, tiled=True).reshape(value.shape)


def local_step(orbitals, potential, unlocked):
    third, first, first_back, special, second, second_back, modes = tables()
    outs = (held(SLAB * 14, 128), held(NB, ROWS, COLS, NG), held(16, NG))
    scratch = [pltpu.SMEM((NB,), jnp.int32)] + [(ROWS + 1, COLS, NB, 128), (ROWS + 1, COLS, NB, 64), (ROWS, COLS, NG), (MODES, NG), (ROWS * WIDE, NG)]
    made = call(forward_third, "hhhh", outs, scratch + [pltpu.SemaphoreType.DMA((2 * ROWS + 3,))])
    spectrum, local, sums = made(unlocked, orbitals.transpose(1, 2, 0, 3), potential, third)
    spectrum = trade(spectrum, "slab", SLAB)
    spectrum = trade(call(forward_first, "kk", held(PENCIL * 12, 128))(spectrum, first), "pencil", PENCIL)
    made = call(middle, "kkkkk", held(PENCIL * 7, 128), [(256, 128), (2 * NB * SLOTS, 256), (16, 128)])
    spectrum = trade(made(spectrum, sums, modes, second, second_back), "pencil", PENCIL)
    made = call(back_first, "kkk", held(SLAB * 7, 128))
    spectrum = trade(made(spectrum, first_back, special), "slab", SLAB)
    made = call(back_third, "kkk", f32(ROWS, COLS, NB, NG), [(MODES, ROWS * HALF)])
    return made(spectrum, local, third).transpose(2, 0, 1, 3)


def solution(mesh):
    in_specs = (P(None, "slab", "pencil", None), P("slab", "pencil", None), P())
    out_specs = P(None, "slab", "pencil", None)
    return jax.shard_map(local_step, mesh=mesh, in_specs=in_specs, out_specs=out_specs, check_vma=False)
```
